32 devices in a mesh: groups: 2 (over x), seq: 16 (over z, y, core).
Axes of the slice: x: 2, y: 2, z: 4, core: 2. Of those that a mesh axis runs over, the one named last changes fastest.
Arguments:
- features: bfloat16 [4, 8192, 768], P('groups', 'seq'), parts along dimension 0, may hold values from -6 to 6
- gain_first: float32 [768], replicated, may hold values from 0.1 to 1.9
- kernel_first: float32 [5, 768], replicated, may hold values from -2.5 to 2.5
- weight_first: bfloat16 [768, 768], replicated, may hold values from -0.21875 to 0.21875
- bias_first: float32 [768], replicated, may hold values from -3 to 3
- gain_second: float32 [768], replicated, may hold values from 0.1 to 1.9
- kernel_second: float32 [5, 768], replicated, may hold values from -2.5 to 2.5
- weight_second: bfloat16 [768, 896], replicated, may hold values from -0.21875 to 0.21875
- bias_second: float32 [896], replicated, may hold values from -3 to 3
- cotangent: bfloat16 [4, 2048, 896], P('groups', 'seq'), parts along dimension 0, may hold values from -6 to 6
Outputs:
- grad_features: bfloat16 [4, 8192, 768], P('groups', 'seq'), parts along dimension 0
- grad_weight_first: float32 [1536, 768], P('groups', 'seq'), parts along dimension 0
- grad_weight_second: float32 [1536, 896], P('groups', 'seq'), parts along dimension 0
- grad_bias_first: float32 [1536], P('groups'), parts along dimension 0
- grad_bias_second: float32 [1792], P('groups'), parts along dimension 0
- grad_kernel_first: float32 [10, 768], P('groups'), parts along dimension 0
- grad_kernel_second: float32 [10, 768], P('groups'), parts along dimension 0
- grad_gain_first: float32 [1536], P('groups'), parts along dimension 0
- grad_gain_second: float32 [1536], P('groups'), parts along dimension 0
The draws below stay inside these ranges and needn't reach their ends.
There are 2 independent parts, one for each index of `groups`. The reference program is written for one: setup_inputs(seed, part) draws one part's arguments, and reference() takes and returns one part's arrays. A program takes and returns all parts, laid end to end along the dimension named above; an argument that names none is the same for every part. Nothing has to cross between parts.
All inputs are finite; a program needn't handle non-finite values.
Results may differ from the reference program's by a relative error of at most 0.0067.
Values may be sent and summed in bfloat16 or wider, within the bound.
A program may use at most 128 MiB of HBM per device.

```python
import math
import jax
import jax.numpy as jnp
from jax import lax

C1 = 768
C2 = 896
TAPS = 5
BATCH = 2
LENGTH = 8192


def spiked(entries, own_key, source, target, blocks, factor):
    owner, partner = [(jnp.arange(entries.shape[position]) // (entries.shape[position] // blocks)).reshape([-1 if axis == position else 1 for axis in range(entries.ndim)]) for position in (source, target)]
    chosen = jax.random.permutation(own_key, blocks)[partner]
    strong = (owner == chosen) | (owner == (partner + blocks // 2) % blocks)
    return jnp.where(strong, factor * entries, entries)


def levels(key, shape, shards, least, largest):
    gain = 1.0
    for dim, shards_of in shards:
        steps = jax.random.uniform(jax.random.fold_in(jax.random.fold_in(key, 6), dim), (shards_of,), jnp.float32, least / len(shards), largest / len(shards))
        gain = gain * jnp.repeat(jnp.exp(steps), shape[dim] // shards_of).reshape((-1,) + (1,) * (len(shape) - 1 - dim))
    return gain


def bell_draw(key, dims, scale, most, pieces=(), kind=jnp.bfloat16):
    result = jax.random.normal(key, dims, jnp.float32) * scale
    if len(pieces) > 0:
        result = levels(key, dims, pieces, -0.22, 0.18) * result
    return jnp.clip(result, min=-most, max=most).astype(kind)


def bell_draw_with(stream_key, dims, deviation, most, cuts, heavy, kind=jnp.bfloat16):
    result = deviation * jax.random.normal(stream_key, dims, jnp.float32)
    if cuts:
        result = result * levels(stream_key, dims, cuts, -0.22, 0.18)
    return jnp.clip(spiked(result, jax.random.fold_in(stream_key, 3), *heavy), -most, most).astype(kind)


def setup_inputs(seed: int = 0, part: int = 0) -> dict:
    key_of = jax.random.split(jax.random.key(seed), 11)
    own_keys = jax.random.split(jax.random.fold_in(key_of[10], part), 11)
    return {
        "features": bell_draw(own_keys[0], (BATCH, LENGTH, C1), 1.0, 6.0, ((1, 16),)),
        "gain_first": jnp.clip(1.0 + 0.18 * jax.random.normal(key_of[1], (C1,), jnp.float32), 0.1, 1.9),
        "kernel_first": bell_draw(key_of[2], (TAPS, C1), TAPS ** -0.5, 2.5, (), jnp.float32),
        "weight_first": bell_draw(key_of[3], (C1, C1), C1 ** -0.5, 0.21875),
        "bias_first": bell_draw(key_of[4], (C1,), 0.5, 3.0, (), jnp.float32),
        "gain_second": jnp.clip(1.0 + 0.18 * jax.random.normal(key_of[5], (C1,), jnp.float32), 0.1, 1.9),
        "kernel_second": bell_draw(key_of[6], (TAPS, C1), TAPS ** -0.5, 2.5, (), jnp.float32),
        "weight_second": bell_draw(key_of[7], (C1, C2), C1 ** -0.5, 0.21875),
        "bias_second": bell_draw(key_of[8], (C2,), 0.5, 3.0, (), jnp.float32),
        "cotangent": bell_draw_with(own_keys[9], (BATCH, LENGTH // 4, C2), 1.0, 6.0, ((1, 16),), (1, 2, 16, 2.0)),
    }


epsilon = 1e-06
inv_sqrt_two = 0.7071067811865476
inv_sqrt_tau = 0.3989422804014327

def gelu_pair(inputs):
    normal_cdf = 0.5 * (1.0 + jax.scipy.special.erf(inputs * inv_sqrt_two))
    density = jnp.exp(-0.5 * inputs * inputs) * inv_sqrt_tau
    return (inputs * normal_cdf, normal_cdf + inputs * density)

def rms_forward(values, gain_vec):
    factor = lax.rsqrt(lax.optimization_barrier(jnp.mean(values * values, axis=-1, keepdims=True)) + epsilon)
    return (values * factor * gain_vec, factor)

def rms_backward(values, factor, gain_vec, grad_norm):
    scaled = grad_norm * gain_vec
    inner = lax.optimization_barrier(jnp.mean(scaled * values, axis=-1, keepdims=True))
    return factor * scaled - values * (factor * factor * factor) * inner

def pad_two(values):
    return jnp.pad(values, ((0, 0), (2, 2), (0, 0)))

def taps_forward(padded, kernel, extent):
    total = kernel[0] * padded[:, 0:extent]
    for offset in range(1, 5):
        total = total + kernel[offset] * padded[:, offset:offset + extent]
    return total

def taps_backward(padded, kernel, extent):
    total = kernel[0] * padded[:, 4:4 + extent]
    for offset in range(1, 5):
        total = total + kernel[offset] * padded[:, 4 - offset:4 - offset + extent]
    return total

def taps_kernel(padded, grad_conv, extent):
    return jnp.stack([lax.optimization_barrier(jnp.sum(padded[:, offset:offset + extent] * grad_conv, axis=(0, 1))) for offset in range(5)])

def project(matrix, weight):
    flat = matrix.reshape(-1, matrix.shape[-1])
    return jnp.dot(flat, weight, preferred_element_type=jnp.float32).reshape(matrix.shape[0], matrix.shape[1], weight.shape[1])

def project_back(matrix, weight):
    flat = matrix.reshape(-1, matrix.shape[-1])
    return jnp.dot(flat, weight.T, preferred_element_type=jnp.float32).reshape(matrix.shape[0], matrix.shape[1], weight.shape[0])

def weight_grad(matrix, other):
    flat_left = matrix.reshape(-1, matrix.shape[-1])
    flat_right = other.reshape(-1, other.shape[-1])
    return lax.dot_general(flat_left, flat_right, (((0,), (0,)), ((), ())), preferred_element_type=jnp.float32)

def pool_pairs(values):
    return (values[:, 0::2] + values[:, 1::2]) * 0.5

def spread_pairs(values):
    return jnp.repeat(values * 0.5, 2, axis=1)

def widen(values):
    return lax.optimization_barrier(values.astype(jnp.bfloat16)).astype(jnp.float32)

def reference(features, gain_first, kernel_first, weight_first, bias_first, gain_second, kernel_second, weight_second, bias_second, cotangent):
    channels = features.shape[2]
    extent = features.shape[1]
    pooled_len = extent // 2
    norm_scale = 1.0 / math.sqrt(features.shape[0] * extent)
    values = features.astype(jnp.float32)
    norm_first, factor_first = rms_forward(values, gain_first)
    norm_first_pad = pad_two(norm_first)
    conv_first = taps_forward(norm_first_pad, kernel_first, extent).astype(jnp.bfloat16)
    pre_first = project(conv_first, weight_first) + bias_first
    act_first, slope_first = gelu_pair(pre_first)
    pooled = pool_pairs(values + act_first).astype(jnp.bfloat16)
    pooled_f = pooled.astype(jnp.float32)
    norm_second, factor_second = rms_forward(pooled_f, gain_second)
    norm_second_pad = pad_two(norm_second)
    conv_second = taps_forward(norm_second_pad, kernel_second, pooled_len).astype(jnp.bfloat16)
    pre_second = project(conv_second, weight_second) + bias_second
    unused, slope_second = gelu_pair(pre_second)
    up_second = spread_pairs(cotangent.astype(jnp.float32))
    back_second = (up_second * slope_second).astype(jnp.bfloat16)
    grad_weight_second = weight_grad(conv_second, back_second) * norm_scale
    grad_bias_second = lax.optimization_barrier(jnp.sum(back_second.astype(jnp.float32), axis=(0, 1))) * norm_scale
    into_second = widen(project_back(back_second, weight_second))
    dnorm_second = taps_backward(pad_two(into_second), kernel_second, pooled_len)
    grad_kernel_second = taps_kernel(norm_second_pad, into_second, pooled_len) * norm_scale
    grad_gain_second = lax.optimization_barrier(jnp.sum(dnorm_second * pooled_f * factor_second, axis=(0, 1))) * norm_scale
    dpooled = rms_backward(pooled_f, factor_second, gain_second, dnorm_second) + up_second[:, :, :channels]
    up_first = spread_pairs(dpooled)
    back_first = (up_first * slope_first).astype(jnp.bfloat16)
    grad_weight_first = weight_grad(conv_first, back_first) * norm_scale
    grad_bias_first = lax.optimization_barrier(jnp.sum(back_first.astype(jnp.float32), axis=(0, 1))) * norm_scale
    into_first = widen(project_back(back_first, weight_first))
    dnorm_first = taps_backward(pad_two(into_first), kernel_first, extent)
    grad_kernel_first = taps_kernel(norm_first_pad, into_first, extent) * norm_scale
    grad_gain_first = lax.optimization_barrier(jnp.sum(dnorm_first * values * factor_first, axis=(0, 1))) * norm_scale
    grad_features = (up_first + rms_backward(values, factor_first, gain_first, dnorm_first)).astype(jnp.bfloat16)
    return (grad_features, grad_weight_first, grad_weight_second, grad_bias_first, grad_bias_second, grad_kernel_first, grad_kernel_second, grad_gain_first, grad_gain_second)
```

```python
import functools
import math

import jax
import jax.numpy as jnp
from jax import lax
from jax.experimental import pallas as pl
from jax.experimental.pallas import tpu as pltpu
from jax.sharding import PartitionSpec as P

MESH = pl.DeviceIdType.MESH
F32 = jnp.float32
BF16 = jnp.bfloat16
epsilon = 1e-06
inv_sqrt_two = 0.7071067811865476
inv_sqrt_tau = 0.3989422804014327
HALO = 16
LANES = 128


def gelu_parts(v):
    cdf = 0.5 * (1.0 + lax.erf(v * inv_sqrt_two))
    return cdf, jnp.exp(-0.5 * v * v) * inv_sqrt_tau


def extend(planes):
    m, rows = len(planes), planes[0].shape[0]
    down = [pltpu.roll(planes[i], 1, 0) for i in (m - 2, m - 1)]
    up = [pltpu.roll(planes[i], rows - 1, 0) for i in (0, 1)]
    return down + planes + up


def halo_kernel(n, x_ref, c_ref, xb_ref, xa_ref, cb_ref, ca_ref, send_sem, recv_sem):
    me = lax.axis_index("seq")
    right, left = lax.rem(me + 1, n), lax.rem(me + n - 1, n)
    barrier = pltpu.get_barrier_semaphore()
    for other in (left, right):
        pl.semaphore_signal(barrier, inc=1, device_id={"seq": other}, device_id_type=MESH)
    pl.semaphore_wait(barrier, 2)
    copies = []
    for ref, before, after in ((x_ref, xb_ref, xa_ref), (c_ref, cb_ref, ca_ref)):
        length = ref.shape[1]
        for source, target, other in (
            (ref.at[:, pl.ds(length - HALO, HALO)], before, right),
            (ref.at[:, pl.ds(0, HALO)], after, left),
        ):
            k = len(copies)
            copies.append(
                pltpu.make_async_remote_copy(
                    src_ref=source,
                    dst_ref=target,
                    send_sem=send_sem.at[k],
                    recv_sem=recv_sem.at[k],
                    device_id={"seq": other},
                    device_id_type=MESH,
                )
            )
            copies[-1].start()
    for copy in copies:
        copy.wait()


def local_kernel(
    scale,
    blocks,
    edge_ref,
    x_ref,
    xb_ref,
    xa_ref,
    c_ref,
    cb_ref,
    ca_ref,
    g1_ref,
    k1_ref,
    w1_ref,
    b1_ref,
    g2_ref,
    k2_ref,
    w2_ref,
    b2_ref,
    out_ref,
    *rest,
):
    if blocks:
        blk_ref, small_ref = rest[:2]
        rest = rest[2:]
    else:
        gt1_ref, gt2_ref, small_ref = rest[:3]
        rest = rest[3:]
    (xs, xp, fac, conv, slope, up, fac2, conv2, back2, own2, into2, cot, ss, own, inside,
     back, own1, into, dn, gt) = rest
    batch, length, ch = x_ref.shape
    ch2 = c_ref.shape[2]
    span = length + 2 * HALO
    per = span // 4
    rows = batch * per
    groups = ch // LANES
    side = HALO // 4

    within = lax.broadcasted_iota(jnp.int32, (rows, LANES), 0)
    for b in range(1, batch):
        within = jnp.where(within >= per, within - per, within)
    is_own = (within >= side) & (within < per - side)
    own[...] = jnp.where(is_own, 1.0, 0.0)
    low = jnp.where(edge_ref[0] == 1, side, 0)
    high = jnp.where(edge_ref[1] == 1, per - side, per)
    inside[...] = jnp.where((within >= low) & (within < high), 1.0, 0.0)
    at_first, at_last = edge_ref[0] == 1, edge_ref[1] == 1

    for b in range(batch):
        base = b * per
        first = cb_ref[b].astype(F32)[HALO - side :] * 0.5
        last = ca_ref[b].astype(F32)[:side] * 0.5
        cot[base : base + side] = jnp.where(at_first, 0.0, first)
        cot[base + side : base + per - side] = c_ref[b].astype(F32) * 0.5
        cot[base + per - side : base + per] = jnp.where(at_last, 0.0, last)

    def lanes(c, width=LANES):
        return pl.ds(pl.multiple_of(c * width, width), width)

    ss[...] = jnp.zeros_like(ss)

    @pl.loop(0, groups)
    def _(c):
        for b in range(batch):
            base = b * span
            xs[c, base : base + HALO] = jnp.where(at_first, 0.0, xb_ref[b, :, lanes(c)].astype(F32))
            xs[c, base + HALO : base + HALO + length] = x_ref[b, :, lanes(c)].astype(F32)
            xs[c, base + HALO + length : base + span] = jnp.where(
                at_last, 0.0, xa_ref[b, :, lanes(c)].astype(F32)
            )
        for r in range(4):
            v = xs[c, pl.ds(r, rows, stride=4), :]
            xp[r * rows : (r + 1) * rows, lanes(c)] = v
            ss[r * rows : (r + 1) * rows] += v * v

    fac[...] = jnp.broadcast_to(
        lax.rsqrt(jnp.sum(ss[...], axis=1, keepdims=True) * (1.0 / ch) + epsilon), fac.shape
    )

    def normed(values, factors, gain_ref, c, m):
        gain = gain_ref[:, lanes(c)]
        return [
            values[r * rows : (r + 1) * rows, lanes(c)] * factors[r * rows : (r + 1) * rows] * gain
            for r in range(m)
        ]

    def taps(c, m, values, factors, gain_ref, kernel_ref, target):
        ext = extend(normed(values, factors, gain_ref, c, m))
        k = [kernel_ref[j : j + 1, lanes(c)] for j in range(5)]
        for r in range(m):
            total = k[0] * ext[r]
            for j in range(1, 5):
                total = total + k[j] * ext[r + j]
            target[r * rows : (r + 1) * rows, lanes(c)] = total.astype(BF16)

    pl.loop(0, groups)(lambda c: taps(c, 4, xp, fac, g1_ref, k1_ref, conv))

    wide = 256

    for t in range(2):

        @pl.loop(0, ch // wide)
        def _(n):
            part = lanes(n, wide)
            pre = jnp.dot(
                conv[2 * t * rows : 2 * (t + 1) * rows], w1_ref[:, part], preferred_element_type=F32
            )
            pre = pre + b1_ref[:, part]
            cdf, density = gelu_parts(pre)
            slope[2 * t * rows : 2 * (t + 1) * rows, part] = cdf + pre * density
            s = xp[2 * t * rows : 2 * (t + 1) * rows, part] + pre * cdf
            pooled = (s[:rows] + s[rows:]) * 0.5
            mask = inside[...]
            mask = jnp.concatenate([mask] * (wide // LANES), axis=1)
            up[t * rows : (t + 1) * rows, part] = (pooled.astype(BF16).astype(F32)) * mask

    total = jnp.zeros((2 * rows, LANES), F32)
    for c in range(groups):
        v = up[:, c * LANES : (c + 1) * LANES]
        total = total + v * v
    fac2[...] = jnp.broadcast_to(
        lax.rsqrt(jnp.sum(total, axis=1, keepdims=True) * (1.0 / ch) + epsilon), fac2.shape
    )
    pl.loop(0, groups)(lambda c: taps(c, 2, up, fac2, g2_ref, k2_ref, conv2))

    @pl.loop(0, ch2 // LANES)
    def _(n):
        part = lanes(n)
        pre = jnp.dot(conv2[...], w2_ref[:, part], preferred_element_type=F32) + b2_ref[:, part]
        cdf, density = gelu_parts(pre)
        grad = cot[:, part]
        total = jnp.zeros((1, LANES), F32)
        for t in range(2):
            at = slice(t * rows, (t + 1) * rows)
            value = (grad * (cdf[at] + pre[at] * density[at])).astype(BF16)
            back2[at, part] = value
            kept = value.astype(F32) * own[...]
            own2[at, part] = kept.astype(BF16)
            total = total + jnp.sum(kept, axis=0, keepdims=True)
        small_ref[14:15, part] = total * scale

    nt = (((1,), (1,)), ((), ()))
    tn = (((0,), (0,)), ((), ()))

    @pl.loop(0, ch // wide)
    def _(n):
        into2[:, lanes(n, wide)] = lax.dot_general(
            back2[...], w2_ref[lanes(n, wide), :], nt, preferred_element_type=F32
        ).astype(BF16)

    def weight_term(left, right, target_rows, offset, plain_ref):
        for s in range(0, left.shape[1], wide):
            e = min(s + wide, left.shape[1])
            gt[s:e] = (
                lax.dot_general(left[:, s:e], right[...], tn, preferred_element_type=F32) * scale
            )
        count = left.shape[1]
        if blocks:
            size = count // 16
            for d in range(16):
                z, y, core = d // 4, (d // 2) % 2, d % 2
                blk_ref[core, y, z, offset : offset + size, :] = gt[
                    d * size : (d + 1) * size
                ].astype(BF16)
        else:
            plain_ref[...] = gt[0:count]

    weight_term(own2, conv2, ch2, ch // 16, None if blocks else gt2_ref)

    def taps_back(c, m, values, factors, gain_ref, kernel_ref, grads, kernel_row, gain_row):
        norm = extend(normed(values, factors, gain_ref, c, m))
        g = [grads[r * rows : (r + 1) * rows, lanes(c)].astype(F32) for r in range(m)]
        ext = extend(g)
        k = [kernel_ref[j : j + 1, lanes(c)] for j in range(5)]
        gain = gain_ref[:, lanes(c)]
        mask = own[...]
        kept = [v * mask for v in g]
        gain_total = jnp.zeros((1, LANES), F32)
        for j in range(5):
            total = norm[j] * kept[0]
            for r in range(1, m):
                total = total + norm[r + j] * kept[r]
            small_ref[kernel_row + j : kernel_row + j + 1, lanes(c)] = (
                jnp.sum(total, axis=0, keepdims=True) * scale
            )
        gain_sum = None
        for r in range(m):
            at = slice(r * rows, (r + 1) * rows)
            d = k[0] * ext[r + 4]
            for j in range(1, 5):
                d = d + k[j] * ext[r + 4 - j]
            v = values[at, lanes(c)]
            dv = d * v
            term = dv * factors[at] * mask
            gain_sum = term if gain_sum is None else gain_sum + term
            ss[at] += dv * gain
            dn[at, lanes(c)] = d * gain
        small_ref[gain_row : gain_row + 1, lanes(c)] = (
            jnp.sum(gain_sum, axis=0, keepdims=True) * scale
        )

    ss[...] = jnp.zeros_like(ss)
    pl.loop(0, groups)(
        lambda c: taps_back(c, 2, up, fac2, g2_ref, k2_ref, into2, 5, 11)
    )
    f2 = fac2[...]
    inner2 = jnp.sum(ss[0 : 2 * rows], axis=1, keepdims=True) * (1.0 / ch)
    ss[0 : 2 * rows] = f2 * f2 * f2 * jnp.broadcast_to(inner2, f2.shape)

    @pl.loop(0, groups)
    def _(c):
        part = lanes(c)
        grad = cot[:, part]
        mask = inside[...] * 0.5
        total = jnp.zeros((1, LANES), F32)
        for t in range(2):
            at = slice(t * rows, (t + 1) * rows)
            d = fac2[at] * dn[at, part] - up[at, part] * ss[at] + grad
            d = d * mask
            up[at, part] = d
            for r in (2 * t, 2 * t + 1):
                to = slice(r * rows, (r + 1) * rows)
                value = (d * slope[to, part]).astype(BF16)
                back[to, part] = value
                kept = value.astype(F32) * own[...]
                own1[to, part] = kept.astype(BF16)
                total = total + jnp.sum(kept, axis=0, keepdims=True)
        small_ref[13:14, part] = total * scale

    @pl.loop(0, ch // wide)
    def _(n):
        into[:, lanes(n, wide)] = lax.dot_general(
            back[...], w1_ref[lanes(n, wide), :], nt, preferred_element_type=F32
        ).astype(BF16)

    weight_term(own1, conv, ch, 0, None if blocks else gt1_ref)

    ss[...] = jnp.zeros_like(ss)
    pl.loop(0, groups)(lambda c: taps_back(c, 4, xp, fac, g1_ref, k1_ref, into, 0, 10))
    f1 = fac[...]
    inner = jnp.sum(ss[...], axis=1, keepdims=True) * (1.0 / ch)
    ss[...] = f1 * f1 * f1 * jnp.broadcast_to(inner, f1.shape)
    small_ref[12:13, :] = jnp.zeros((1, small_ref.shape[1]), F32)
    small_ref[15:16, :] = jnp.zeros((1, small_ref.shape[1]), F32)
    small_ref[0:14, ch:] = jnp.zeros((14, small_ref.shape[1] - ch), F32)

    @pl.loop(0, groups)
    def _(c):
        part = lanes(c)
        for r in range(4):
            at = slice(r * rows, (r + 1) * rows)
            half = slice((r // 2) * rows, (r // 2 + 1) * rows)
            v = up[half, part] + fac[at] * dn[at, part] - xp[at, part] * ss[at]
            xs[c, pl.ds(r, rows, stride=4), :] = v
        for b in range(batch):
            base = b * span + HALO
            out_ref[b, :, part] = xs[c, base : base + length].astype(BF16)


def sum_kernel(blk, small, out_ref, small_out, recv1, kept, send2, recv2, send3, recv3, total,
               srecv1, ssend2, srecv2, sall, send_sem, recv_sem):
    g = lax.axis_index("seq")
    z, y, c = g // 4, lax.rem(g // 2, 2), lax.rem(g, 2)
    core = g + 1 - 2 * c
    over = g + 2 - 4 * y

    def hop(step):
        zt = lax.rem(z + step, 4)
        return zt, zt * 4 + y * 2 + c

    barrier = pltpu.get_barrier_semaphore()
    others = [core, over] + [hop(s)[1] for s in (1, 2, 3)]
    for other in others:
        pl.semaphore_signal(barrier, inc=1, device_id={"seq": other}, device_id_type=MESH)
    pl.semaphore_wait(barrier, 5)

    def send(k, source, target, other):
        copy = pltpu.make_async_remote_copy(
            src_ref=source,
            dst_ref=target,
            send_sem=send_sem.at[k],
            recv_sem=recv_sem.at[k],
            device_id={"seq": other},
            device_id_type=MESH,
        )
        copy.start()
        return copy

    small1 = send(0, small, srecv1, core)
    far = send(1, blk.at[1 - c, 1 - y], recv1.at[0], core)
    near = send(2, blk.at[1 - c, y], recv1.at[1], core)

    far.wait()
    steps = (2, 1, 3, 0)
    over_copies = []
    for i, step in enumerate(steps):
        zt, _ = hop(step)
        send2[i] = (blk[c, 1 - y, zt].astype(F32) + recv1[0, zt].astype(F32)).astype(BF16)
        over_copies.append(send(3 + i, send2.at[i], recv2.at[i], over))
        if i == 0:
            small1.wait()
            ssend2[...] = small[...] + srecv1[...]
            small2 = send(7, ssend2, srecv2, over)
    near.wait()
    for i, step in enumerate(steps):
        zt, _ = hop(step)
        kept[i] = blk[c, y, zt].astype(F32) + recv1[1, zt].astype(F32)

    z_copies = []
    for i, step in enumerate(steps):
        over_copies[i].wait()
        if i == 0:
            small2.wait()
            sall[z] = ssend2[...] + srecv2[...]
        if step:
            _, other = hop(step)
            send3[i] = (kept[i] + recv2[i].astype(F32)).astype(BF16)
            z_copies.append(send(8 + i, send3.at[i], recv3.at[i], other))
            z_copies.append(send(11 + i, sall.at[z], sall.at[z], other))
        else:
            total[...] = kept[i] + recv2[i].astype(F32)
    for copy in z_copies:
        copy.wait()
    result = total[...]
    for i in range(3):
        result = result + recv3[i].astype(F32)
    out_ref[...] = result
    small_out[...] = (sall[0] + sall[1]) + (sall[2] + sall[3])


def per_device(fast, n, x, g1, k1, w1, b1, g2, k2, w2, b2, cot):
    batch, length, ch = x.shape
    quarter, ch2 = cot.shape[1:]
    scale = 1.0 / math.sqrt(batch * length * n)
    any_spec = pl.BlockSpec(memory_space=pl.ANY)
    vmem = pl.BlockSpec(memory_space=pltpu.VMEM)

    xb, xa, cb, ca = pl.pallas_call(
        functools.partial(halo_kernel, n),
        out_shape=[jax.ShapeDtypeStruct((batch, HALO, ch), BF16)] * 2
        + [jax.ShapeDtypeStruct((batch, HALO, ch2), BF16)] * 2,
        in_specs=[any_spec] * 2,
        out_specs=[any_spec] * 4,
        scratch_shapes=[pltpu.SemaphoreType.DMA((4,)), pltpu.SemaphoreType.DMA((4,))],
        compiler_params=pltpu.CompilerParams(collective_id=0, has_side_effects=True),
        name="halo",
    )(x, cot)

    me = lax.axis_index("seq")
    edge = jnp.stack([me == 0, me == n - 1]).astype(jnp.int32)
    rows = batch * (length + 2 * HALO) // 4
    lead = (ch + ch2) // 16
    if fast:
        grads = [jax.ShapeDtypeStruct((2, 2, 4, lead, ch), BF16)]
    else:
        grads = [jax.ShapeDtypeStruct((ch, ch), F32), jax.ShapeDtypeStruct((ch2, ch), F32)]
    outs = pl.pallas_call(
        functools.partial(local_kernel, scale, fast),
        out_shape=[jax.ShapeDtypeStruct(x.shape, BF16)]
        + grads
        + [jax.ShapeDtypeStruct((16, ch2), F32)],
        in_specs=[pl.BlockSpec(memory_space=pltpu.SMEM)] + [vmem] * 14,
        out_specs=[vmem] * (2 + len(grads)),
        scratch_shapes=[
            pltpu.VMEM((ch // LANES, 4 * rows, LANES), F32),
            pltpu.VMEM((4 * rows, ch), F32),
            pltpu.VMEM((4 * rows, LANES), F32),
            pltpu.VMEM((4 * rows, ch), BF16),
            pltpu.VMEM((4 * rows, ch), F32),
            pltpu.VMEM((2 * rows, ch), F32),
            pltpu.VMEM((2 * rows, LANES), F32),
            pltpu.VMEM((2 * rows, ch), BF16),
            pltpu.VMEM((2 * rows, ch2), BF16),
            pltpu.VMEM((2 * rows, ch2), BF16),
            pltpu.VMEM((2 * rows, ch), BF16),
            pltpu.VMEM((rows, ch2), F32),
            pltpu.VMEM((4 * rows, LANES), F32),
            pltpu.VMEM((rows, LANES), F32),
            pltpu.VMEM((rows, LANES), F32),
            pltpu.VMEM((4 * rows, ch), BF16),
            pltpu.VMEM((4 * rows, ch), BF16),
            pltpu.VMEM((4 * rows, ch), BF16),
            pltpu.VMEM((4 * rows, ch), F32),
            pltpu.VMEM((max(ch, ch2), ch), F32),
        ],
        compiler_params=pltpu.CompilerParams(vmem_limit_bytes=56 * 2**20),
        name="local",
    )(
        edge, x, xb, xa, cot, cb, ca,
        g1[None], k1, w1, b1[None], g2[None], k2, w2, b2[None],
    )
    grad_x = outs[0]
    if fast:
        _, blk, small = outs
        total, small = pl.pallas_call(
            sum_kernel,
            out_shape=[
                jax.ShapeDtypeStruct((lead, ch), F32),
                jax.ShapeDtypeStruct(small.shape, F32),
            ],
            in_specs=[vmem] * 2,
            out_specs=[vmem] * 2,
            scratch_shapes=[
                pltpu.VMEM((2, 4, lead, ch), BF16),
                pltpu.VMEM((4, lead, ch), F32),
                pltpu.VMEM((4, lead, ch), BF16),
                pltpu.VMEM((4, lead, ch), BF16),
                pltpu.VMEM((3, lead, ch), BF16),
                pltpu.VMEM((3, lead, ch), BF16),
                pltpu.VMEM((lead, ch), F32),
                pltpu.VMEM(small.shape, F32),
                pltpu.VMEM(small.shape, F32),
                pltpu.VMEM(small.shape, F32),
                pltpu.VMEM((4,) + small.shape, F32),
                pltpu.SemaphoreType.DMA((14,)),
                pltpu.SemaphoreType.DMA((14,)),
            ],
            compiler_params=pltpu.CompilerParams(
                collective_id=1, has_side_effects=True, vmem_limit_bytes=40 * 2**20
            ),
            name="sums",
        )(blk, small)
        grad_w1, grad_w2 = total[: ch // 16].T, total[ch // 16 :].T
    else:
        _, gt1, gt2, small = outs
        grad_w1 = lax.psum_scatter(gt1, "seq", scatter_dimension=0, tiled=True).T
        grad_w2 = lax.psum_scatter(gt2, "seq", scatter_dimension=0, tiled=True).T
        small = lax.psum(small, "seq")
    return (
        grad_x,
        grad_w1,
        grad_w2,
        small[13, :ch],
        small[14],
        small[0:5, :ch],
        small[5:10, :ch],
        small[10, :ch],
        small[11, :ch],
    )


def solution(mesh):
    n = mesh.shape["seq"]
    return jax.shard_map(
        functools.partial(per_device, n == 16, n),
        mesh=mesh,
        in_specs=(P("groups", "seq", None),) + (P(),) * 8 + (P("groups", "seq", None),),
        out_specs=(
            P("groups", "seq", None),
            P("groups", "seq"),
            P("groups", "seq"),
            P("groups"),
            P("groups"),
            P("groups", None),
            P("groups", None),
            P("groups"),
            P("groups"),
        ),
        check_vma=False,
    )
```

```python
import functools
import math

import jax
import jax.numpy as jnp
from jax import lax
from jax.experimental import pallas as pl
from jax.experimental.pallas import tpu as pltpu
from jax.sharding import PartitionSpec as P

MESH = pl.DeviceIdType.MESH
F32 = jnp.float32
BF16 = jnp.bfloat16
epsilon = 1e-06
inv_sqrt_two = 0.7071067811865476
inv_sqrt_tau = 0.3989422804014327
HALO = 16
LANES = 128


def gelu_parts(v):
    cdf = 0.5 * (1.0 + lax.erf(v * inv_sqrt_two))
    return cdf, jnp.exp(-0.5 * v * v) * inv_sqrt_tau


def extend(planes):
    m, rows = len(planes), planes[0].shape[0]
    down = [pltpu.roll(planes[i], 1, 0) for i in (m - 2, m - 1)]
    up = [pltpu.roll(planes[i], rows - 1, 0) for i in (0, 1)]
    return down + planes + up


def step_kernel(
    scale,
    n,
    blocks,
    x_ref,
    g1_in,
    k1_ref,
    w1_hbm,
    b1_in,
    g2_in,
    k2_ref,
    w2_hbm,
    b2_in,
    c_ref,
    out_ref,
    *rest,
):
    if blocks:
        sum1_ref, sum2_ref, small_out = rest[:3]
    else:
        gt1_ref, gt2_ref, small_out = rest[:3]
    (xs, xp, fac, conv, slope, up, fac2, conv2, back2, own2, into2, cot, ss, own, inside,
     back, own1, into, dn, gt, xb_ref, xa_ref, cb_ref, ca_ref, w1_ref, w2_ref,
     g1_ref, b1_ref, g2_ref, b2_ref, small_ref, halo_send, halo_recv, load_sem) = rest[3:37]
    rest = rest[37:]
    batch, length, ch = x_ref.shape
    ch2 = c_ref.shape[2]
    span = length + 2 * HALO
    per = span // 4
    rows = batch * per
    groups = ch // LANES
    side = HALO // 4

    me = lax.axis_index("seq")
    right, left = lax.rem(me + 1, n), lax.rem(me + n - 1, n)
    others = [left, right]
    if blocks:
        z, y, core = me // 4, lax.rem(me // 2, 2), lax.rem(me, 2)
        hops = [(lax.rem(z + s, 4), lax.rem(z + s, 4) * 4 + y * 2 + core) for s in range(4)]
        mate, over = me + 1 - 2 * core, me + 2 - 4 * y
        others += [mate, over] + [hops[s][1] for s in (1, 2, 3)]
    loads = [
        pltpu.make_async_copy(w1_hbm, w1_ref, load_sem.at[0]),
        pltpu.make_async_copy(w2_hbm, w2_ref, load_sem.at[1]),
    ]
    barrier = pltpu.get_barrier_semaphore()
    for other in others:
        pl.semaphore_signal(barrier, inc=1, device_id={"seq": other}, device_id_type=MESH)
    for load in loads:
        load.start()
    for source, target in ((g1_in, g1_ref), (b1_in, b1_ref), (g2_in, g2_ref), (b2_in, b2_ref)):
        target[...] = source[...].reshape(target.shape)
    pl.semaphore_wait(barrier, len(others))

    def send(source, target, sems, k, other):
        copy = pltpu.make_async_remote_copy(
            src_ref=source,
            dst_ref=target,
            send_sem=sems[0].at[k],
            recv_sem=sems[1].at[k],
            device_id={"seq": other},
            device_id_type=MESH,
        )
        copy.start()
        return copy

    halo = []
    for ref, before, after in ((x_ref, xb_ref, xa_ref), (c_ref, cb_ref, ca_ref)):
        last = ref.shape[1] - HALO
        for source, target, other in (
            (ref.at[:, pl.ds(last, HALO)], before, right),
            (ref.at[:, pl.ds(0, HALO)], after, left),
        ):
            halo.append(send(source, target, (halo_send, halo_recv), len(halo), other))

    within = lax.broadcasted_iota(jnp.int32, (rows, LANES), 0)
    for b in range(1, batch):
        within = jnp.where(within >= per, within - per, within)
    is_own = (within >= side) & (within < per - side)
    own[...] = jnp.where(is_own, 1.0, 0.0)
    at_first, at_last = me == 0, me == n - 1
    low = jnp.where(at_first, side, 0)
    high = jnp.where(at_last, per - side, per)
    inside[...] = jnp.where((within >= low) & (within < high), 1.0, 0.0)
    def lanes(c, width=LANES):
        return pl.ds(pl.multiple_of(c * width, width), width)

    ss[...] = jnp.zeros_like(ss)
    small_ref[...] = jnp.zeros_like(small_ref)

    @pl.loop(0, groups)
    def _(c):
        for b in range(batch):
            base = b * span + HALO
            xs[c, base : base + length] = x_ref[b, :, lanes(c)].astype(F32)

    for b in range(batch):
        cot[b * per + side : (b + 1) * per - side] = c_ref[b].astype(F32) * 0.5
    for copy in halo:
        copy.wait()

    for b in range(batch):
        base = b * per
        first = cb_ref[b].astype(F32)[HALO - side :] * 0.5
        last = ca_ref[b].astype(F32)[:side] * 0.5
        cot[base : base + side] = jnp.where(at_first, 0.0, first)
        cot[base + per - side : base + per] = jnp.where(at_last, 0.0, last)


    @pl.loop(0, groups)
    def _(c):
        for b in range(batch):
            base = b * span
            xs[c, base : base + HALO] = jnp.where(at_first, 0.0, xb_ref[b, :, lanes(c)].astype(F32))
            xs[c, base + HALO + length : base + span] = jnp.where(
                at_last, 0.0, xa_ref[b, :, lanes(c)].astype(F32)
            )
        for r in range(4):
            v = xs[c, pl.ds(r, rows, stride=4), :]
            xp[r * rows : (r + 1) * rows, lanes(c)] = v
            ss[r * rows : (r + 1) * rows] += v * v

    fac[...] = jnp.broadcast_to(
        lax.rsqrt(jnp.sum(ss[...], axis=1, keepdims=True) * (1.0 / ch) + epsilon), fac.shape
    )

    def normed(values, factors, gain_ref, c, m):
        gain = gain_ref[:, lanes(c)]
        return [
            values[r * rows : (r + 1) * rows, lanes(c)] * factors[r * rows : (r + 1) * rows] * gain
            for r in range(m)
        ]

    def taps(c, m, values, factors, gain_ref, kernel_ref, target):
        ext = extend(normed(values, factors, gain_ref, c, m))
        k = [kernel_ref[j : j + 1, lanes(c)] for j in range(5)]
        for r in range(m):
            total = k[0] * ext[r]
            for j in range(1, 5):
                total = total + k[j] * ext[r + j]
            target[r * rows : (r + 1) * rows, lanes(c)] = total.astype(BF16)

    pl.loop(0, groups)(lambda c: taps(c, 4, xp, fac, g1_ref, k1_ref, conv))

    for load in loads:
        load.wait()

    wide = 256

    for t in range(2):

        @pl.loop(0, ch // wide)
        def _(n):
            part = lanes(n, wide)
            pre = jnp.dot(
                conv[2 * t * rows : 2 * (t + 1) * rows], w1_ref[:, part], preferred_element_type=F32
            )
            pre = pre + b1_ref[:, part]
            cdf, density = gelu_parts(pre)
            slope[2 * t * rows : 2 * (t + 1) * rows, part] = cdf + pre * density
            s = xp[2 * t * rows : 2 * (t + 1) * rows, part] + pre * cdf
            pooled = (s[:rows] + s[rows:]) * 0.5
            mask = inside[...]
            mask = jnp.concatenate([mask] * (wide // LANES), axis=1)
            up[t * rows : (t + 1) * rows, part] = (pooled.astype(BF16).astype(F32)) * mask

    total = jnp.zeros((2 * rows, LANES), F32)
    for c in range(groups):
        v = up[:, c * LANES : (c + 1) * LANES]
        total = total + v * v
    fac2[...] = jnp.broadcast_to(
        lax.rsqrt(jnp.sum(total, axis=1, keepdims=True) * (1.0 / ch) + epsilon), fac2.shape
    )
    pl.loop(0, groups)(lambda c: taps(c, 2, up, fac2, g2_ref, k2_ref, conv2))

    @pl.loop(0, ch2 // LANES)
    def _(n):
        part = lanes(n)
        pre = jnp.dot(conv2[...], w2_ref[:, part], preferred_element_type=F32) + b2_ref[:, part]
        cdf, density = gelu_parts(pre)
        grad = cot[:, part]
        total = jnp.zeros((1, LANES), F32)
        for t in range(2):
            at = slice(t * rows, (t + 1) * rows)
            value = (grad * (cdf[at] + pre[at] * density[at])).astype(BF16)
            back2[at, part] = value
            kept = value.astype(F32) * own[...]
            own2[at, part] = kept.astype(BF16)
            total = total + jnp.sum(kept, axis=0, keepdims=True)
        small_ref[14:15, part] = total * scale

    nt = (((1,), (1,)), ((), ()))
    tn = (((0,), (0,)), ((), ()))

    @pl.loop(0, ch // wide)
    def _(n):
        into2[:, lanes(n, wide)] = lax.dot_general(
            back2[...], w2_ref[lanes(n, wide), :], nt, preferred_element_type=F32
        ).astype(BF16)

    def weight_term(left, right, plain_ref, blk):
        for s in range(0, left.shape[1], wide):
            e = min(s + wide, left.shape[1])
            gt[s:e] = (
                lax.dot_general(left[:, s:e], right[...], tn, preferred_element_type=F32) * scale
            )
        count = left.shape[1]
        if blocks:
            size = count // 16
            for d in range(16):
                blk[d % 2, (d // 2) % 2, d // 4] = gt[d * size : (d + 1) * size].astype(BF16)
        else:
            plain_ref[...] = gt[0:count]

    if blocks:
        sums = (rest[0:9], rest[9:18])
        srecv1, ssend2, srecv2, sall, small_send, small_recv = rest[18:24]
        steps = (2, 1, 3, 0)
        flight = {}

        def stage_core(m):
            blk, recv1, sems = sums[m][0], sums[m][1], sums[m][7:9]
            flight[m] = [
                send(blk.at[1 - core, 1 - y], recv1.at[0], sems, 0, mate),
                send(blk.at[1 - core, y], recv1.at[1], sems, 1, mate),
            ]

        def stage_y(m):
            blk, recv1, kept, send2, recv2 = sums[m][:5]
            far, near = flight[m]
            far.wait()
            moving = []
            for i, step in enumerate(steps):
                zt = hops[step][0]
                send2[i] = (blk[core, 1 - y, zt].astype(F32) + recv1[0, zt].astype(F32)).astype(BF16)
                moving.append(send(send2.at[i], recv2.at[i], sums[m][7:9], 2 + i, over))
            near.wait()
            for i, step in enumerate(steps):
                zt = hops[step][0]
                kept[i] = blk[core, y, zt].astype(F32) + recv1[1, zt].astype(F32)
            flight[m] = moving

        def stage_z(m):
            kept, recv2, send3, recv3 = sums[m][2], sums[m][4], sums[m][5], sums[m][6]
            moving = []
            for i, step in enumerate(steps):
                flight[m][i].wait()
                if step:
                    send3[i] = (kept[i] + recv2[i].astype(F32)).astype(BF16)
                    moving.append(
                        send(send3.at[i], recv3.at[i], sums[m][7:9], 6 + i, hops[step][1])
                    )
                else:
                    kept[i] = kept[i] + recv2[i].astype(F32)
            flight[m] = moving

        def stage_end(m, target):
            kept, recv3 = sums[m][2], sums[m][6]
            for copy in flight[m]:
                copy.wait()
            target[...] = (kept[3] + recv3[0].astype(F32)) + (
                recv3[1].astype(F32) + recv3[2].astype(F32)
            )

    weight_term(own2, conv2, None if blocks else gt2_ref, sums[1][0] if blocks else None)
    if blocks:
        stage_core(1)

    def taps_back(c, m, values, factors, gain_ref, kernel_ref, grads, kernel_row, gain_row):
        norm = extend(normed(values, factors, gain_ref, c, m))
        g = [grads[r * rows : (r + 1) * rows, lanes(c)].astype(F32) for r in range(m)]
        ext = extend(g)
        k = [kernel_ref[j : j + 1, lanes(c)] for j in range(5)]
        gain = gain_ref[:, lanes(c)]
        mask = own[...]
        kept = [v * mask for v in g]
        gain_total = jnp.zeros((1, LANES), F32)
        for j in range(5):
            total = norm[j] * kept[0]
            for r in range(1, m):
                total = total + norm[r + j] * kept[r]
            small_ref[kernel_row + j : kernel_row + j + 1, lanes(c)] = (
                jnp.sum(total, axis=0, keepdims=True) * scale
            )
        gain_sum = None
        for r in range(m):
            at = slice(r * rows, (r + 1) * rows)
            d = k[0] * ext[r + 4]
            for j in range(1, 5):
                d = d + k[j] * ext[r + 4 - j]
            v = values[at, lanes(c)]
            dv = d * v
            term = dv * factors[at] * mask
            gain_sum = term if gain_sum is None else gain_sum + term
            ss[at] += dv * gain
            dn[at, lanes(c)] = d * gain
        small_ref[gain_row : gain_row + 1, lanes(c)] = (
            jnp.sum(gain_sum, axis=0, keepdims=True) * scale
        )

    ss[...] = jnp.zeros_like(ss)
    pl.loop(0, groups)(
        lambda c: taps_back(c, 2, up, fac2, g2_ref, k2_ref, into2, 5, 11)
    )
    f2 = fac2[...]
    inner2 = jnp.sum(ss[0 : 2 * rows], axis=1, keepdims=True) * (1.0 / ch)
    ss[0 : 2 * rows] = f2 * f2 * f2 * jnp.broadcast_to(inner2, f2.shape)

    if blocks:
        stage_y(1)

    @pl.loop(0, groups)
    def _(c):
        part = lanes(c)
        grad = cot[:, part]
        mask = inside[...] * 0.5
        total = jnp.zeros((1, LANES), F32)
        for t in range(2):
            at = slice(t * rows, (t + 1) * rows)
            d = fac2[at] * dn[at, part] - up[at, part] * ss[at] + grad
            d = d * mask
            up[at, part] = d
            for r in (2 * t, 2 * t + 1):
                to = slice(r * rows, (r + 1) * rows)
                value = (d * slope[to, part]).astype(BF16)
                back[to, part] = value
                kept = value.astype(F32) * own[...]
                own1[to, part] = kept.astype(BF16)
                total = total + jnp.sum(kept, axis=0, keepdims=True)
        small_ref[13:14, part] = total * scale

    weight_term(own1, conv, None if blocks else gt1_ref, sums[0][0] if blocks else None)
    if blocks:
        stage_core(0)

    @pl.loop(0, ch // wide)
    def _(n):
        into[:, lanes(n, wide)] = lax.dot_general(
            back[...], w1_ref[lanes(n, wide), :], nt, preferred_element_type=F32
        ).astype(BF16)

    if blocks:
        stage_z(1)
        stage_y(0)

    ss[...] = jnp.zeros_like(ss)
    pl.loop(0, groups)(lambda c: taps_back(c, 4, xp, fac, g1_ref, k1_ref, into, 0, 10))
    if blocks:
        small_sems = (small_send, small_recv)
        small_move = send(small_ref, srecv1, small_sems, 0, mate)
        stage_z(0)
    f1 = fac[...]
    inner = jnp.sum(ss[...], axis=1, keepdims=True) * (1.0 / ch)
    ss[...] = f1 * f1 * f1 * jnp.broadcast_to(inner, f1.shape)
    def finish(c):
        part = lanes(c)
        for r in range(4):
            at = slice(r * rows, (r + 1) * rows)
            half = slice((r // 2) * rows, (r // 2 + 1) * rows)
            v = up[half, part] + fac[at] * dn[at, part] - xp[at, part] * ss[at]
            xs[c, pl.ds(r, rows, stride=4), :] = v
        for b in range(batch):
            base = b * span + HALO
            out_ref[b, :, part] = xs[c, base : base + length].astype(BF16)

    middle = groups // 2
    pl.loop(0, middle)(finish)
    if blocks:
        small_move.wait()
        ssend2[...] = small_ref[...] + srecv1[...]
        small_move = send(ssend2, srecv2, small_sems, 1, over)
    pl.loop(middle, groups)(finish)
    if blocks:
        small_move.wait()
        sall[z] = ssend2[...] + srecv2[...]
        small_moves = [
            send(sall.at[z], sall.at[z], small_sems, 1 + s, hops[s][1]) for s in (1, 2, 3)
        ]
        stage_end(1, sum2_ref)
        stage_end(0, sum1_ref)
        for copy in small_moves:
            copy.wait()
        small_out[...] = (sall[0] + sall[1]) + (sall[2] + sall[3])
    else:
        small_out[...] = small_ref[...]


def sums_scratch(ch, ch2, small_shape):
    shapes = []
    for size in (ch // 16, ch2 // 16):
        shapes += [
            pltpu.VMEM((2, 2, 4, size, ch), BF16),
            pltpu.VMEM((2, 4, size, ch), BF16),
            pltpu.VMEM((4, size, ch), F32),
            pltpu.VMEM((4, size, ch), BF16),
            pltpu.VMEM((4, size, ch), BF16),
            pltpu.VMEM((3, size, ch), BF16),
            pltpu.VMEM((3, size, ch), BF16),
            pltpu.SemaphoreType.DMA((9,)),
            pltpu.SemaphoreType.DMA((9,)),
        ]
    shapes += [pltpu.VMEM(small_shape, F32)] * 3 + [pltpu.VMEM((4,) + small_shape, F32)]
    return shapes + [pltpu.SemaphoreType.DMA((5,)), pltpu.SemaphoreType.DMA((5,))]


def per_device(fast, n, x, g1, k1, w1, b1, g2, k2, w2, b2, cot):
    batch, length, ch = x.shape
    quarter, ch2 = cot.shape[1:]
    scale = 1.0 / math.sqrt(batch * length * n)
    any_spec = pl.BlockSpec(memory_space=pl.ANY)
    vmem = pl.BlockSpec(memory_space=pltpu.VMEM)

    rows = batch * (length + 2 * HALO) // 4
    small_shape = (16, ch2)
    if fast:
        grads = [jax.ShapeDtypeStruct((k // 16, ch), F32) for k in (ch, ch2)]
    else:
        grads = [jax.ShapeDtypeStruct((ch, ch), F32), jax.ShapeDtypeStruct((ch2, ch), F32)]
    outs = pl.pallas_call(
        functools.partial(step_kernel, scale, n, fast),
        out_shape=[jax.ShapeDtypeStruct(x.shape, BF16)]
        + grads
        + [jax.ShapeDtypeStruct(small_shape, F32)],
        in_specs=[vmem] * 3 + [any_spec] + [vmem] * 3 + [any_spec] + [vmem] * 2,
        out_specs=[vmem] * (2 + len(grads)),
        scratch_shapes=[
            pltpu.VMEM((ch // LANES, 4 * rows, LANES), F32),
            pltpu.VMEM((4 * rows, ch), F32),
            pltpu.VMEM((4 * rows, LANES), F32),
            pltpu.VMEM((4 * rows, ch), BF16),
            pltpu.VMEM((4 * rows, ch), F32),
            pltpu.VMEM((2 * rows, ch), F32),
            pltpu.VMEM((2 * rows, LANES), F32),
            pltpu.VMEM((2 * rows, ch), BF16),
            pltpu.VMEM((2 * rows, ch2), BF16),
            pltpu.VMEM((2 * rows, ch2), BF16),
            pltpu.VMEM((2 * rows, ch), BF16),
            pltpu.VMEM((rows, ch2), F32),
            pltpu.VMEM((4 * rows, LANES), F32),
            pltpu.VMEM((rows, LANES), F32),
            pltpu.VMEM((rows, LANES), F32),
            pltpu.VMEM((4 * rows, ch), BF16),
            pltpu.VMEM((4 * rows, ch), BF16),
            pltpu.VMEM((4 * rows, ch), BF16),
            pltpu.VMEM((4 * rows, ch), F32),
            pltpu.VMEM((max(ch, ch2), ch), F32),
            pltpu.VMEM((batch, HALO, ch), BF16),
            pltpu.VMEM((batch, HALO, ch), BF16),
            pltpu.VMEM((batch, HALO, ch2), BF16),
            pltpu.VMEM((batch, HALO, ch2), BF16),
            pltpu.VMEM(w1.shape, BF16),
            pltpu.VMEM(w2.shape, BF16),
            pltpu.VMEM((1, ch), F32),
            pltpu.VMEM((1, ch), F32),
            pltpu.VMEM((1, ch), F32),
            pltpu.VMEM((1, ch2), F32),
            pltpu.VMEM(small_shape, F32),
            pltpu.SemaphoreType.DMA((4,)),
            pltpu.SemaphoreType.DMA((4,)),
            pltpu.SemaphoreType.DMA((2,)),
        ]
        + (sums_scratch(ch, ch2, small_shape) if fast else []),
        compiler_params=pltpu.CompilerParams(
            collective_id=0, has_side_effects=True, vmem_limit_bytes=58 * 2**20
        ),
        name="step",
    )(x, g1, k1, w1, b1, g2, k2, w2, b2, cot)
    grad_x, *parts, small = outs
    if fast:
        grad_w1, grad_w2 = parts[0].T, parts[1].T
    else:
        grad_w1, grad_w2 = [
            lax.psum_scatter(part, "seq", scatter_dimension=0, tiled=True).T for part in parts
        ]
        small = lax.psum(small, "seq")
    return (
        grad_x,
        grad_w1,
        grad_w2,
        small[13, :ch],
        small[14],
        small[0:5, :ch],
        small[5:10, :ch],
        small[10, :ch],
        small[11, :ch],
    )


def solution(mesh):
    n = mesh.shape["seq"]
    return jax.shard_map(
        functools.partial(per_device, n == 16, n),
        mesh=mesh,
        in_specs=(P("groups", "seq", None),) + (P(),) * 8 + (P("groups", "seq", None),),
        out_specs=(
            P("groups", "seq", None),
            P("groups", "seq"),
            P("groups", "seq"),
            P("groups"),
            P("groups"),
            P("groups", None),
            P("groups", None),
            P("groups"),
            P("groups"),
        ),
        check_vma=False,
    )
```

```python
import functools
import math

import jax
import jax.numpy as jnp
from jax import lax
from jax.experimental import pallas as pl
from jax.experimental.pallas import tpu as pltpu
from jax.sharding import PartitionSpec as P

MESH = pl.DeviceIdType.MESH
F32 = jnp.float32
BF16 = jnp.bfloat16
epsilon = 1e-06
inv_sqrt_two = 0.7071067811865476
inv_sqrt_tau = 0.3989422804014327
HALO = 16
LANES = 128


def gelu_parts(v):
    cdf = 0.5 * (1.0 + lax.erf(v * inv_sqrt_two))
    return cdf, jnp.exp(-0.5 * v * v) * inv_sqrt_tau


def extend(planes):
    m, rows = len(planes), planes[0].shape[0]
    down = [pltpu.roll(planes[i], 1, 0) for i in (m - 2, m - 1)]
    up = [pltpu.roll(planes[i], rows - 1, 0) for i in (0, 1)]
    return down + planes + up


def step_kernel(
    scale,
    n,
    blocks,
    x_ref,
    g1_in,
    k1_ref,
    w1_hbm,
    b1_in,
    g2_in,
    k2_ref,
    w2_hbm,
    b2_in,
    c_ref,
    out_ref,
    *rest,
):
    if blocks:
        sum1_ref, sum2_ref, small_out = rest[:3]
    else:
        gt1_ref, gt2_ref, small_out = rest[:3]
    (xs, xp, fac, conv, slope, up, fac2, conv2, back2, own2, into2, cot, ss, own, inside,
     back, own1, into, dn, gt, xb_ref, xa_ref, cb_ref, ca_ref, w1_ref, w2_ref,
     g1_ref, b1_ref, g2_ref, b2_ref, small_ref, halo_send, halo_recv, load_sem) = rest[3:37]
    rest = rest[37:]
    batch, length, ch = x_ref.shape
    ch2 = c_ref.shape[2]
    span = length + 2 * HALO
    per = span // 4
    rows = batch * per
    groups = ch // LANES
    side = HALO // 4

    me = lax.axis_index("seq")
    right, left = lax.rem(me + 1, n), lax.rem(me + n - 1, n)
    others = [left, right]
    if blocks:
        z, y, core = me // 4, lax.rem(me // 2, 2), lax.rem(me, 2)
        hops = [(lax.rem(z + s, 4), lax.rem(z + s, 4) * 4 + y * 2 + core) for s in range(4)]
        mate, over = me + 1 - 2 * core, me + 2 - 4 * y
        others += [mate, over] + [hops[s][1] for s in (1, 2, 3)]
    loads = [
        pltpu.make_async_copy(w1_hbm, w1_ref, load_sem.at[0]),
        pltpu.make_async_copy(w2_hbm, w2_ref, load_sem.at[1]),
    ]
    barrier = pltpu.get_barrier_semaphore()
    for other in others:
        pl.semaphore_signal(barrier, inc=1, device_id={"seq": other}, device_id_type=MESH)
    for load in loads:
        load.start()
    for source, target in ((g1_in, g1_ref), (b1_in, b1_ref), (g2_in, g2_ref), (b2_in, b2_ref)):
        target[...] = source[...].reshape(target.shape)
    pl.semaphore_wait(barrier, len(others))

    def remote(source, target, sems, k, other):
        return pltpu.make_async_remote_copy(
            src_ref=source,
            dst_ref=target,
            send_sem=sems[0].at[k],
            recv_sem=sems[1].at[k],
            device_id={"seq": other},
            device_id_type=MESH,
        )

    def send(*args):
        copy = remote(*args)
        copy.start()
        return copy

    halo = []
    for ref, before, after in ((x_ref, xb_ref, xa_ref), (c_ref, cb_ref, ca_ref)):
        last = ref.shape[1] - HALO
        for source, target, other in (
            (ref.at[:, pl.ds(last, HALO)], before, right),
            (ref.at[:, pl.ds(0, HALO)], after, left),
        ):
            halo.append(send(source, target, (halo_send, halo_recv), len(halo), other))

    within = lax.broadcasted_iota(jnp.int32, (rows, LANES), 0)
    for b in range(1, batch):
        within = jnp.where(within >= per, within - per, within)
    is_own = (within >= side) & (within < per - side)
    own[...] = jnp.where(is_own, 1.0, 0.0)
    at_first, at_last = me == 0, me == n - 1
    low = jnp.where(at_first, side, 0)
    high = jnp.where(at_last, per - side, per)
    inside[...] = jnp.where((within >= low) & (within < high), 1.0, 0.0)
    def lanes(c, width=LANES):
        return pl.ds(pl.multiple_of(c * width, width), width)

    ss[...] = jnp.zeros_like(ss)
    small_ref[...] = jnp.zeros_like(small_ref)

    @pl.loop(0, groups)
    def _(c):
        for b in range(batch):
            base = b * span + HALO
            xs[c, base : base + length] = x_ref[b, :, lanes(c)].astype(F32)

    for b in range(batch):
        cot[b * per + side : (b + 1) * per - side] = c_ref[b].astype(F32) * 0.5
    for copy in halo:
        copy.wait()

    for b in range(batch):
        base = b * per
        first = cb_ref[b].astype(F32)[HALO - side :] * 0.5
        last = ca_ref[b].astype(F32)[:side] * 0.5
        cot[base : base + side] = jnp.where(at_first, 0.0, first)
        cot[base + per - side : base + per] = jnp.where(at_last, 0.0, last)


    @pl.loop(0, groups)
    def _(c):
        for b in range(batch):
            base = b * span
            xs[c, base : base + HALO] = jnp.where(at_first, 0.0, xb_ref[b, :, lanes(c)].astype(F32))
            xs[c, base + HALO + length : base + span] = jnp.where(
                at_last, 0.0, xa_ref[b, :, lanes(c)].astype(F32)
            )
        for r in range(4):
            v = xs[c, pl.ds(r, rows, stride=4), :]
            xp[r * rows : (r + 1) * rows, lanes(c)] = v
            ss[r * rows : (r + 1) * rows] += v * v

    fac[...] = jnp.broadcast_to(
        lax.rsqrt(jnp.sum(ss[...], axis=1, keepdims=True) * (1.0 / ch) + epsilon), fac.shape
    )

    def normed(values, factors, gain_ref, c, m):
        gain = gain_ref[:, lanes(c)]
        return [
            values[r * rows : (r + 1) * rows, lanes(c)] * factors[r * rows : (r + 1) * rows] * gain
            for r in range(m)
        ]

    def taps(c, m, values, factors, gain_ref, kernel_ref, target):
        ext = extend(normed(values, factors, gain_ref, c, m))
        k = [kernel_ref[j : j + 1, lanes(c)] for j in range(5)]
        for r in range(m):
            total = k[0] * ext[r]
            for j in range(1, 5):
                total = total + k[j] * ext[r + j]
            target[r * rows : (r + 1) * rows, lanes(c)] = total.astype(BF16)

    pl.loop(0, groups)(lambda c: taps(c, 4, xp, fac, g1_ref, k1_ref, conv))

    for load in loads:
        load.wait()

    wide = 256

    for t in range(2):

        @pl.loop(0, ch // wide)
        def _(n):
            part = lanes(n, wide)
            pre = jnp.dot(
                conv[2 * t * rows : 2 * (t + 1) * rows], w1_ref[:, part], preferred_element_type=F32
            )
            pre = pre + b1_ref[:, part]
            cdf, density = gelu_parts(pre)
            slope[2 * t * rows : 2 * (t + 1) * rows, part] = cdf + pre * density
            s = xp[2 * t * rows : 2 * (t + 1) * rows, part] + pre * cdf
            pooled = (s[:rows] + s[rows:]) * 0.5
            mask = inside[...]
            mask = jnp.concatenate([mask] * (wide // LANES), axis=1)
            up[t * rows : (t + 1) * rows, part] = (pooled.astype(BF16).astype(F32)) * mask

    total = jnp.zeros((2 * rows, LANES), F32)
    for c in range(groups):
        v = up[:, c * LANES : (c + 1) * LANES]
        total = total + v * v
    fac2[...] = jnp.broadcast_to(
        lax.rsqrt(jnp.sum(total, axis=1, keepdims=True) * (1.0 / ch) + epsilon), fac2.shape
    )
    pl.loop(0, groups)(lambda c: taps(c, 2, up, fac2, g2_ref, k2_ref, conv2))

    @pl.loop(0, ch2 // LANES)
    def _(n):
        part = lanes(n)
        pre = jnp.dot(conv2[...], w2_ref[:, part], preferred_element_type=F32) + b2_ref[:, part]
        cdf, density = gelu_parts(pre)
        grad = cot[:, part]
        total = jnp.zeros((1, LANES), F32)
        for t in range(2):
            at = slice(t * rows, (t + 1) * rows)
            value = (grad * (cdf[at] + pre[at] * density[at])).astype(BF16)
            back2[at, part] = value
            kept = value.astype(F32) * own[...]
            own2[at, part] = kept.astype(BF16)
            total = total + jnp.sum(kept, axis=0, keepdims=True)
        small_ref[14:15, part] = total * scale

    nt = (((1,), (1,)), ((), ()))
    tn = (((0,), (0,)), ((), ()))

    @pl.loop(0, ch // wide)
    def _(n):
        into2[:, lanes(n, wide)] = lax.dot_general(
            back2[...], w2_ref[lanes(n, wide), :], nt, preferred_element_type=F32
        ).astype(BF16)

    def weight_term(left, right, plain_ref, blk):
        for s in range(0, left.shape[1], wide):
            e = min(s + wide, left.shape[1])
            gt[s:e] = (
                lax.dot_general(left[:, s:e], right[...], tn, preferred_element_type=F32) * scale
            )
        count = left.shape[1]
        if blocks:
            size = count // 16
            for d in range(16):
                blk[d % 2, (d // 2) % 2, d // 4] = gt[d * size : (d + 1) * size].astype(BF16)
        else:
            plain_ref[...] = gt[0:count]

    if blocks:
        sums = (rest[0:9], rest[9:18])
        srecv1, ssend2, srecv2, sall, small_send, small_recv = rest[18:24]
        steps = (2, 1, 3, 0)
        flight = {}

        def stage_core(m):
            blk, recv1, sems = sums[m][0], sums[m][1], sums[m][7:9]
            flight[m] = [
                send(blk.at[1 - core, 1 - y], recv1.at[0], sems, 0, mate),
                send(blk.at[1 - core, y], recv1.at[1], sems, 1, mate),
            ]

        def stage_y(m):
            blk, recv1, kept, send2, recv2 = sums[m][:5]
            far, near = flight[m]
            far.wait()
            for i, step in enumerate(steps):
                zt = hops[step][0]
                send2[i] = (blk[core, 1 - y, zt].astype(F32) + recv1[0, zt].astype(F32)).astype(BF16)
                send(send2.at[i], recv2.at[i], sums[m][7:9], 2 + i, over)
            near.wait()
            for i, step in enumerate(steps):
                zt = hops[step][0]
                kept[i] = blk[core, y, zt].astype(F32) + recv1[1, zt].astype(F32)

        def z_copy(m, i):
            send3, recv3, sems = sums[m][5], sums[m][6], sums[m][7:9]
            return remote(send3.at[i], recv3.at[i], sems, 6 + i, hops[steps[i]][1])

        def stage_z(m, i):
            kept, recv2, send3 = sums[m][2], sums[m][4], sums[m][5]
            remote(sums[m][3].at[i], recv2.at[i], sums[m][7:9], 2 + i, over).wait()
            if steps[i]:
                send3[i] = (kept[i] + recv2[i].astype(F32)).astype(BF16)
                z_copy(m, i).start()
            else:
                kept[i] = kept[i] + recv2[i].astype(F32)

        def stage_end(m, target):
            kept, recv3 = sums[m][2], sums[m][6]
            for i in range(3):
                z_copy(m, i).wait()
            target[...] = (kept[3] + recv3[0].astype(F32)) + (
                recv3[1].astype(F32) + recv3[2].astype(F32)
            )

    weight_term(own2, conv2, None if blocks else gt2_ref, sums[1][0] if blocks else None)
    if blocks:
        stage_core(1)

    def taps_back(c, m, values, factors, gain_ref, kernel_ref, grads, kernel_row, gain_row):
        norm = extend(normed(values, factors, gain_ref, c, m))
        g = [grads[r * rows : (r + 1) * rows, lanes(c)].astype(F32) for r in range(m)]
        ext = extend(g)
        k = [kernel_ref[j : j + 1, lanes(c)] for j in range(5)]
        gain = gain_ref[:, lanes(c)]
        mask = own[...]
        kept = [v * mask for v in g]
        gain_total = jnp.zeros((1, LANES), F32)
        for j in range(5):
            total = norm[j] * kept[0]
            for r in range(1, m):
                total = total + norm[r + j] * kept[r]
            small_ref[kernel_row + j : kernel_row + j + 1, lanes(c)] = (
                jnp.sum(total, axis=0, keepdims=True) * scale
            )
        gain_sum = None
        for r in range(m):
            at = slice(r * rows, (r + 1) * rows)
            d = k[0] * ext[r + 4]
            for j in range(1, 5):
                d = d + k[j] * ext[r + 4 - j]
            v = values[at, lanes(c)]
            dv = d * v
            term = dv * factors[at] * mask
            gain_sum = term if gain_sum is None else gain_sum + term
            ss[at] += dv * gain
            dn[at, lanes(c)] = d * gain
        small_ref[gain_row : gain_row + 1, lanes(c)] = (
            jnp.sum(gain_sum, axis=0, keepdims=True) * scale
        )

    ss[...] = jnp.zeros_like(ss)
    pl.loop(0, groups)(
        lambda c: taps_back(c, 2, up, fac2, g2_ref, k2_ref, into2, 5, 11)
    )
    f2 = fac2[...]
    inner2 = jnp.sum(ss[0 : 2 * rows], axis=1, keepdims=True) * (1.0 / ch)
    ss[0 : 2 * rows] = f2 * f2 * f2 * jnp.broadcast_to(inner2, f2.shape)

    if blocks:
        stage_y(1)

    @pl.loop(0, groups)
    def _(c):
        part = lanes(c)
        grad = cot[:, part]
        mask = inside[...] * 0.5
        total = jnp.zeros((1, LANES), F32)
        for t in range(2):
            at = slice(t * rows, (t + 1) * rows)
            d = fac2[at] * dn[at, part] - up[at, part] * ss[at] + grad
            d = d * mask
            up[at, part] = d
            for r in (2 * t, 2 * t + 1):
                to = slice(r * rows, (r + 1) * rows)
                value = (d * slope[to, part]).astype(BF16)
                back[to, part] = value
                kept = value.astype(F32) * own[...]
                own1[to, part] = kept.astype(BF16)
                total = total + jnp.sum(kept, axis=0, keepdims=True)
        small_ref[13:14, part] = total * scale

    weight_term(own1, conv, None if blocks else gt1_ref, sums[0][0] if blocks else None)
    if blocks:
        stage_core(0)

    @pl.loop(0, ch // wide)
    def _(n):
        into[:, lanes(n, wide)] = lax.dot_general(
            back[...], w1_ref[lanes(n, wide), :], nt, preferred_element_type=F32
        ).astype(BF16)

    if blocks:
        for i in range(4):
            stage_z(1, i)
        stage_y(0)

    ss[...] = jnp.zeros_like(ss)

    @pl.loop(0, groups)
    def _(c):
        taps_back(c, 4, xp, fac, g1_ref, k1_ref, into, 0, 10)
        if blocks:
            for i in range(4):
                pl.when(c == groups - 4 + i)(functools.partial(stage_z, 0, i))

    if blocks:
        small_sems = (small_send, small_recv)
        small_move = send(small_ref, srecv1, small_sems, 0, mate)
    f1 = fac[...]
    inner = jnp.sum(ss[...], axis=1, keepdims=True) * (1.0 / ch)
    ss[...] = f1 * f1 * f1 * jnp.broadcast_to(inner, f1.shape)
    def finish(c):
        part = lanes(c)
        for r in range(4):
            at = slice(r * rows, (r + 1) * rows)
            half = slice((r // 2) * rows, (r // 2 + 1) * rows)
            v = up[half, part] + fac[at] * dn[at, part] - xp[at, part] * ss[at]
            out_ref[at, part] = v.astype(BF16)

    middle = groups // 2
    pl.loop(0, middle)(finish)
    if blocks:
        small_move.wait()
        ssend2[...] = small_ref[...] + srecv1[...]
        small_move = send(ssend2, srecv2, small_sems, 1, over)
    pl.loop(middle, groups)(finish)
    if blocks:
        small_move.wait()
        sall[z] = ssend2[...] + srecv2[...]
        small_moves = [
            send(sall.at[z], sall.at[z], small_sems, 1 + s, hops[s][1]) for s in (1, 2, 3)
        ]
        stage_end(1, sum2_ref)
        stage_end(0, sum1_ref)
        for copy in small_moves:
            copy.wait()
        small_out[...] = (sall[0] + sall[1]) + (sall[2] + sall[3])
    else:
        small_out[...] = small_ref[...]


def tail_kernel(fast, p_ref, small_ref, *refs):
    if fast:
        s1_ref, s2_ref, x_out, w1_out, w2_out = refs[:5]
        refs = refs[5:]
    else:
        x_out, refs = refs[0], refs[1:]
    b1_out, b2_out, k1_out, k2_out, g1_out, g2_out, mix = refs
    batch, length, width = x_out.shape
    rows = p_ref.shape[0] // 4
    span = 4 * rows // batch
    ch = b1_out.shape[0]

    @pl.when(pl.program_id(0) == 0)
    def _():
        if fast:
            w1_out[...] = s1_ref[...]
            w2_out[...] = s2_ref[...]
        b1_out[...] = small_ref[13, :ch]
        b2_out[...] = small_ref[14, :]
        k1_out[...] = small_ref[0:5, :ch]
        k2_out[...] = small_ref[5:10, :ch]
        g1_out[...] = small_ref[10, :ch]
        g2_out[...] = small_ref[11, :ch]

    for k in range(width // LANES):
        part = slice(k * LANES, (k + 1) * LANES)
        for r in range(4):
            mix[k, pl.ds(r, rows, stride=4), :] = p_ref[r * rows : (r + 1) * rows, part].astype(F32)
        for b in range(batch):
            base = b * span + HALO
            x_out[b, :, part] = mix[k, base : base + length].astype(BF16)


def sums_scratch(ch, ch2, small_shape):
    shapes = []
    for size in (ch // 16, ch2 // 16):
        shapes += [
            pltpu.VMEM((2, 2, 4, size, ch), BF16),
            pltpu.VMEM((2, 4, size, ch), BF16),
            pltpu.VMEM((4, size, ch), F32),
            pltpu.VMEM((4, size, ch), BF16),
            pltpu.VMEM((4, size, ch), BF16),
            pltpu.VMEM((3, size, ch), BF16),
            pltpu.VMEM((3, size, ch), BF16),
            pltpu.SemaphoreType.DMA((9,)),
            pltpu.SemaphoreType.DMA((9,)),
        ]
    shapes += [pltpu.VMEM(small_shape, F32)] * 3 + [pltpu.VMEM((4,) + small_shape, F32)]
    return shapes + [pltpu.SemaphoreType.DMA((5,)), pltpu.SemaphoreType.DMA((5,))]


def per_device(fast, n, x, g1, k1, w1, b1, g2, k2, w2, b2, cot):
    batch, length, ch = x.shape
    quarter, ch2 = cot.shape[1:]
    scale = 1.0 / math.sqrt(batch * length * n)
    any_spec = pl.BlockSpec(memory_space=pl.ANY)
    vmem = pl.BlockSpec(memory_space=pltpu.VMEM)

    rows = batch * (length + 2 * HALO) // 4
    small_shape = (16, ch2)
    if fast:
        grads = [jax.ShapeDtypeStruct((k // 16, ch), F32) for k in (ch, ch2)]
    else:
        grads = [jax.ShapeDtypeStruct((ch, ch), F32), jax.ShapeDtypeStruct((ch2, ch), F32)]
    outs = pl.pallas_call(
        functools.partial(step_kernel, scale, n, fast),
        out_shape=[jax.ShapeDtypeStruct((4 * rows, ch), BF16)]
        + grads
        + [jax.ShapeDtypeStruct(small_shape, F32)],
        in_specs=[vmem] * 3 + [any_spec] + [vmem] * 3 + [any_spec] + [vmem] * 2,
        out_specs=[vmem] * (2 + len(grads)),
        scratch_shapes=[
            pltpu.VMEM((ch // LANES, 4 * rows, LANES), F32),
            pltpu.VMEM((4 * rows, ch), F32),
            pltpu.VMEM((4 * rows, LANES), F32),
            pltpu.VMEM((4 * rows, ch), BF16),
            pltpu.VMEM((4 * rows, ch), F32),
            pltpu.VMEM((2 * rows, ch), F32),
            pltpu.VMEM((2 * rows, LANES), F32),
            pltpu.VMEM((2 * rows, ch), BF16),
            pltpu.VMEM((2 * rows, ch2), BF16),
            pltpu.VMEM((2 * rows, ch2), BF16),
            pltpu.VMEM((2 * rows, ch), BF16),
            pltpu.VMEM((rows, ch2), F32),
            pltpu.VMEM((4 * rows, LANES), F32),
            pltpu.VMEM((rows, LANES), F32),
            pltpu.VMEM((rows, LANES), F32),
            pltpu.VMEM((4 * rows, ch), BF16),
            pltpu.VMEM((4 * rows, ch), BF16),
            pltpu.VMEM((4 * rows, ch), BF16),
            pltpu.VMEM((4 * rows, ch), F32),
            pltpu.VMEM((max(ch, ch2), ch), F32),
            pltpu.VMEM((batch, HALO, ch), BF16),
            pltpu.VMEM((batch, HALO, ch), BF16),
            pltpu.VMEM((batch, HALO, ch2), BF16),
            pltpu.VMEM((batch, HALO, ch2), BF16),
            pltpu.VMEM(w1.shape, BF16),
            pltpu.VMEM(w2.shape, BF16),
            pltpu.VMEM((1, ch), F32),
            pltpu.VMEM((1, ch), F32),
            pltpu.VMEM((1, ch), F32),
            pltpu.VMEM((1, ch2), F32),
            pltpu.VMEM(small_shape, F32),
            pltpu.SemaphoreType.DMA((4,)),
            pltpu.SemaphoreType.DMA((4,)),
            pltpu.SemaphoreType.DMA((2,)),
        ]
        + (sums_scratch(ch, ch2, small_shape) if fast else []),
        compiler_params=pltpu.CompilerParams(
            collective_id=0, has_side_effects=True, vmem_limit_bytes=58 * 2**20
        ),
        name="step",
    )(x, g1, k1, w1, b1, g2, k2, w2, b2, cot)
    planes, *parts, small = outs
    if not fast:
        grad_w = [
            lax.psum_scatter(part, "seq", scatter_dimension=0, tiled=True).T for part in parts
        ]
        small = lax.psum(small, "seq")
        parts = []

    def whole(shape):
        return pl.BlockSpec(shape, lambda i: (0,) * len(shape))

    width = 2 * LANES
    results = [part.shape for part in parts]
    results += [(ch,), (ch2,), (5, ch), (5, ch), (ch,), (ch,)]
    grad_x, *rest = pl.pallas_call(
        functools.partial(tail_kernel, fast),
        grid=(ch // width,),
        out_shape=[jax.ShapeDtypeStruct(x.shape, BF16)]
        + [jax.ShapeDtypeStruct(shape, F32) for shape in results],
        in_specs=[pl.BlockSpec((4 * rows, width), lambda i: (0, i)), whole(small_shape)]
        + [whole(part.shape) for part in parts],
        out_specs=[pl.BlockSpec((batch, length, width), lambda i: (0, 0, i))]
        + [whole(shape) for shape in results],
        scratch_shapes=[pltpu.VMEM((width // LANES, 4 * rows, LANES), F32)],
        name="tail",
    )(planes, small, *parts)
    if fast:
        grad_w, rest = [part.T for part in rest[:2]], rest[2:]
    return (grad_x, *grad_w, *rest)


def solution(mesh):
    n = mesh.shape["seq"]
    return jax.shard_map(
        functools.partial(per_device, n == 16, n),
        mesh=mesh,
        in_specs=(P("groups", "seq", None),) + (P(),) * 8 + (P("groups", "seq", None),),
        out_specs=(
            P("groups", "seq", None),
            P("groups", "seq"),
            P("groups", "seq"),
            P("groups"),
            P("groups"),
            P("groups", None),
            P("groups", None),
            P("groups"),
            P("groups"),
        ),
        check_vma=False,
    )
```

```python
import functools
import math

import jax
import jax.numpy as jnp
from jax import lax
from jax.experimental import pallas as pl
from jax.experimental.pallas import tpu as pltpu
from jax.sharding import PartitionSpec as P

MESH = pl.DeviceIdType.MESH
F32 = jnp.float32
BF16 = jnp.bfloat16
epsilon = 1e-06
inv_sqrt_two = 0.7071067811865476
inv_sqrt_tau = 0.3989422804014327
HALO = 16
LANES = 128


def gelu_parts(v):
    cdf = 0.5 * (1.0 + lax.erf(v * inv_sqrt_two))
    return cdf, jnp.exp(-0.5 * v * v) * inv_sqrt_tau


def extend(planes):
    m, rows = len(planes), planes[0].shape[0]
    down = [pltpu.roll(planes[i], 1, 0) for i in (m - 2, m - 1)]
    up = [pltpu.roll(planes[i], rows - 1, 0) for i in (0, 1)]
    return down + planes + up


def step_kernel(
    scale,
    n,
    blocks,
    x_ref,
    g1_in,
    k1_ref,
    w1_hbm,
    b1_in,
    g2_in,
    k2_ref,
    w2_hbm,
    b2_in,
    c_ref,
    out_ref,
    *rest,
):
    if blocks:
        sum1_ref, sum2_ref, small_out = rest[:3]
    else:
        gt1_ref, gt2_ref, small_out = rest[:3]
    (xs, xp, fac, conv, slope, up, fac2, conv2, back2, own2, into2, cot, ss, own, inside,
     back, own1, into, dn, gt, xb_ref, xa_ref, cb_ref, ca_ref, w1_ref, w2_ref,
     g1_ref, b1_ref, g2_ref, b2_ref, small_ref, halo_send, halo_recv, load_sem) = rest[3:37]
    rest = rest[37:]
    batch, length, ch = x_ref.shape
    ch2 = c_ref.shape[2]
    span = length + 2 * HALO
    per = span // 4
    rows = batch * per
    groups = ch // LANES
    side = HALO // 4

    me = lax.axis_index("seq")
    right, left = lax.rem(me + 1, n), lax.rem(me + n - 1, n)
    others = [left, right]
    if blocks:
        z, y, core = me // 4, lax.rem(me // 2, 2), lax.rem(me, 2)
        hops = [(lax.rem(z + s, 4), lax.rem(z + s, 4) * 4 + y * 2 + core) for s in range(4)]
        mate, over = me + 1 - 2 * core, me + 2 - 4 * y
        others += [mate, over] + [hops[s][1] for s in (1, 2, 3)]
    loads = [
        pltpu.make_async_copy(w1_hbm, w1_ref, load_sem.at[0]),
        pltpu.make_async_copy(w2_hbm, w2_ref, load_sem.at[1]),
    ]
    barrier = pltpu.get_barrier_semaphore()
    for other in others:
        pl.semaphore_signal(barrier, inc=1, device_id={"seq": other}, device_id_type=MESH)
    for load in loads:
        load.start()
    for source, target in ((g1_in, g1_ref), (b1_in, b1_ref), (g2_in, g2_ref), (b2_in, b2_ref)):
        target[...] = source[...].reshape(target.shape)
    pl.semaphore_wait(barrier, len(others))

    def remote(source, target, sems, k, other):
        return pltpu.make_async_remote_copy(
            src_ref=source,
            dst_ref=target,
            send_sem=sems[0].at[k],
            recv_sem=sems[1].at[k],
            device_id={"seq": other},
            device_id_type=MESH,
        )

    def send(*args):
        copy = remote(*args)
        copy.start()
        return copy

    halo = []
    for ref, before, after in ((x_ref, xb_ref, xa_ref), (c_ref, cb_ref, ca_ref)):
        last = ref.shape[1] - HALO
        for source, target, other in (
            (ref.at[:, pl.ds(last, HALO)], before, right),
            (ref.at[:, pl.ds(0, HALO)], after, left),
        ):
            halo.append(send(source, target, (halo_send, halo_recv), len(halo), other))

    within = lax.broadcasted_iota(jnp.int32, (rows, LANES), 0)
    for b in range(1, batch):
        within = jnp.where(within >= per, within - per, within)
    is_own = (within >= side) & (within < per - side)
    own[...] = jnp.where(is_own, 1.0, 0.0)
    at_first, at_last = me == 0, me == n - 1
    low = jnp.where(at_first, side, 0)
    high = jnp.where(at_last, per - side, per)
    inside[...] = jnp.where((within >= low) & (within < high), 1.0, 0.0)
    def lanes(c, width=LANES):
        return pl.ds(pl.multiple_of(c * width, width), width)

    ss[...] = jnp.zeros_like(ss)
    small_ref[...] = jnp.zeros_like(small_ref)

    @pl.loop(0, groups)
    def _(c):
        for b in range(batch):
            base = b * span + HALO
            xs[c, base : base + length] = x_ref[b, :, lanes(c)].astype(F32)

    for b in range(batch):
        cot[b * per + side : (b + 1) * per - side] = c_ref[b].astype(F32) * 0.5
    for copy in halo:
        copy.wait()

    for b in range(batch):
        base = b * per
        first = cb_ref[b].astype(F32)[HALO - side :] * 0.5
        last = ca_ref[b].astype(F32)[:side] * 0.5
        cot[base : base + side] = jnp.where(at_first, 0.0, first)
        cot[base + per - side : base + per] = jnp.where(at_last, 0.0, last)


    @pl.loop(0, groups)
    def _(c):
        for b in range(batch):
            base = b * span
            xs[c, base : base + HALO] = jnp.where(at_first, 0.0, xb_ref[b, :, lanes(c)].astype(F32))
            xs[c, base + HALO + length : base + span] = jnp.where(
                at_last, 0.0, xa_ref[b, :, lanes(c)].astype(F32)
            )
        for r in range(4):
            v = xs[c, pl.ds(r, rows, stride=4), :]
            xp[r * rows : (r + 1) * rows, lanes(c)] = v
            ss[r * rows : (r + 1) * rows] += v * v

    fac[...] = jnp.broadcast_to(
        lax.rsqrt(jnp.sum(ss[...], axis=1, keepdims=True) * (1.0 / ch) + epsilon), fac.shape
    )

    def normed(values, factors, gain_ref, c, m):
        gain = gain_ref[:, lanes(c)]
        return [
            values[r * rows : (r + 1) * rows, lanes(c)] * factors[r * rows : (r + 1) * rows] * gain
            for r in range(m)
        ]

    def taps(c, m, values, factors, gain_ref, kernel_ref, target):
        ext = extend(normed(values, factors, gain_ref, c, m))
        k = [kernel_ref[j : j + 1, lanes(c)] for j in range(5)]
        for r in range(m):
            total = k[0] * ext[r]
            for j in range(1, 5):
                total = total + k[j] * ext[r + j]
            target[r * rows : (r + 1) * rows, lanes(c)] = total.astype(BF16)

    pl.loop(0, groups)(lambda c: taps(c, 4, xp, fac, g1_ref, k1_ref, conv))

    for load in loads:
        load.wait()

    wide = 256

    for t in range(2):

        @pl.loop(0, ch // wide)
        def _(n):
            part = lanes(n, wide)
            pre = jnp.dot(
                conv[2 * t * rows : 2 * (t + 1) * rows], w1_ref[:, part], preferred_element_type=F32
            )
            pre = pre + b1_ref[:, part]
            cdf, density = gelu_parts(pre)
            slope[2 * t * rows : 2 * (t + 1) * rows, part] = cdf + pre * density
            s = xp[2 * t * rows : 2 * (t + 1) * rows, part] + pre * cdf
            pooled = (s[:rows] + s[rows:]) * 0.5
            mask = inside[...]
            mask = jnp.concatenate([mask] * (wide // LANES), axis=1)
            up[t * rows : (t + 1) * rows, part] = (pooled.astype(BF16).astype(F32)) * mask

    total = jnp.zeros((2 * rows, LANES), F32)
    for c in range(groups):
        v = up[:, c * LANES : (c + 1) * LANES]
        total = total + v * v
    fac2[...] = jnp.broadcast_to(
        lax.rsqrt(jnp.sum(total, axis=1, keepdims=True) * (1.0 / ch) + epsilon), fac2.shape
    )
    pl.loop(0, groups)(lambda c: taps(c, 2, up, fac2, g2_ref, k2_ref, conv2))

    @pl.loop(0, ch2 // LANES)
    def _(n):
        part = lanes(n)
        pre = jnp.dot(conv2[...], w2_ref[:, part], preferred_element_type=F32) + b2_ref[:, part]
        cdf, density = gelu_parts(pre)
        grad = cot[:, part]
        total = jnp.zeros((1, LANES), F32)
        for t in range(2):
            at = slice(t * rows, (t + 1) * rows)
            value = (grad * (cdf[at] + pre[at] * density[at])).astype(BF16)
            back2[at, part] = value
            kept = value.astype(F32) * own[...]
            own2[at, part] = kept.astype(BF16)
            total = total + jnp.sum(kept, axis=0, keepdims=True)
        small_ref[14:15, part] = total * scale

    nt = (((1,), (1,)), ((), ()))
    tn = (((0,), (0,)), ((), ()))

    def weight_term(left, right, plain_ref, blk):
        for s in range(0, left.shape[1], wide):
            e = min(s + wide, left.shape[1])
            gt[s:e] = (
                lax.dot_general(left[:, s:e], right[...], tn, preferred_element_type=F32) * scale
            )
        count = left.shape[1]
        if blocks:
            size = count // 16
            for d in range(16):
                blk[d % 2, (d // 2) % 2, d // 4] = gt[d * size : (d + 1) * size].astype(BF16)
        else:
            plain_ref[...] = gt[0:count]

    if blocks:
        sums = (rest[0:9], rest[9:18])
        srecv1, ssend2, srecv2, sall, small_send, small_recv = rest[18:24]
        steps = (2, 1, 3, 0)
        flight = {}

        def stage_core(m):
            blk, recv1, sems = sums[m][0], sums[m][1], sums[m][7:9]
            flight[m] = [
                send(blk.at[1 - core, 1 - y], recv1.at[0], sems, 0, mate),
                send(blk.at[1 - core, y], recv1.at[1], sems, 1, mate),
            ]

        def stage_y(m):
            blk, recv1, kept, send2, recv2 = sums[m][:5]
            far, near = flight[m]
            far.wait()
            for i, step in enumerate(steps):
                zt = hops[step][0]
                send2[i] = (blk[core, 1 - y, zt].astype(F32) + recv1[0, zt].astype(F32)).astype(BF16)
                send(send2.at[i], recv2.at[i], sums[m][7:9], 2 + i, over)
            near.wait()
            for i, step in enumerate(steps):
                zt = hops[step][0]
                kept[i] = blk[core, y, zt].astype(F32) + recv1[1, zt].astype(F32)

        def z_copy(m, i):
            send3, recv3, sems = sums[m][5], sums[m][6], sums[m][7:9]
            return remote(send3.at[i], recv3.at[i], sems, 6 + i, hops[steps[i]][1])

        def stage_z(m, i):
            kept, recv2, send3 = sums[m][2], sums[m][4], sums[m][5]
            remote(sums[m][3].at[i], recv2.at[i], sums[m][7:9], 2 + i, over).wait()
            if steps[i]:
                send3[i] = (kept[i] + recv2[i].astype(F32)).astype(BF16)
                z_copy(m, i).start()
            else:
                kept[i] = kept[i] + recv2[i].astype(F32)

        def stage_end(m, target):
            kept, recv3 = sums[m][2], sums[m][6]
            for i in range(3):
                z_copy(m, i).wait()
            target[...] = (kept[3] + recv3[0].astype(F32)) + (
                recv3[1].astype(F32) + recv3[2].astype(F32)
            )

    weight_term(own2, conv2, None if blocks else gt2_ref, sums[1][0] if blocks else None)
    if blocks:
        stage_core(1)

    @pl.loop(0, ch // wide)
    def _(n):
        into2[:, lanes(n, wide)] = lax.dot_general(
            back2[...], w2_ref[lanes(n, wide), :], nt, preferred_element_type=F32
        ).astype(BF16)

    if blocks:
        stage_y(1)

    def taps_back(c, m, values, factors, gain_ref, kernel_ref, grads, kernel_row, gain_row):
        norm = extend(normed(values, factors, gain_ref, c, m))
        g = [grads[r * rows : (r + 1) * rows, lanes(c)].astype(F32) for r in range(m)]
        ext = extend(g)
        k = [kernel_ref[j : j + 1, lanes(c)] for j in range(5)]
        gain = gain_ref[:, lanes(c)]
        mask = own[...]
        kept = [v * mask for v in g]
        gain_total = jnp.zeros((1, LANES), F32)
        for j in range(5):
            total = norm[j] * kept[0]
            for r in range(1, m):
                total = total + norm[r + j] * kept[r]
            small_ref[kernel_row + j : kernel_row + j + 1, lanes(c)] = (
                jnp.sum(total, axis=0, keepdims=True) * scale
            )
        gain_sum = None
        for r in range(m):
            at = slice(r * rows, (r + 1) * rows)
            d = k[0] * ext[r + 4]
            for j in range(1, 5):
                d = d + k[j] * ext[r + 4 - j]
            v = values[at, lanes(c)]
            dv = d * v
            term = dv * factors[at] * mask
            gain_sum = term if gain_sum is None else gain_sum + term
            ss[at] += dv * gain
            dn[at, lanes(c)] = d * gain
        small_ref[gain_row : gain_row + 1, lanes(c)] = (
            jnp.sum(gain_sum, axis=0, keepdims=True) * scale
        )

    ss[...] = jnp.zeros_like(ss)
    pl.loop(0, groups)(
        lambda c: taps_back(c, 2, up, fac2, g2_ref, k2_ref, into2, 5, 11)
    )
    f2 = fac2[...]
    inner2 = jnp.sum(ss[0 : 2 * rows], axis=1, keepdims=True) * (1.0 / ch)
    ss[0 : 2 * rows] = f2 * f2 * f2 * jnp.broadcast_to(inner2, f2.shape)

    @pl.loop(0, groups)
    def _(c):
        part = lanes(c)
        grad = cot[:, part]
        mask = inside[...] * 0.5
        total = jnp.zeros((1, LANES), F32)
        for t in range(2):
            at = slice(t * rows, (t + 1) * rows)
            d = fac2[at] * dn[at, part] - up[at, part] * ss[at] + grad
            d = d * mask
            up[at, part] = d
            for r in (2 * t, 2 * t + 1):
                to = slice(r * rows, (r + 1) * rows)
                value = (d * slope[to, part]).astype(BF16)
                back[to, part] = value
                kept = value.astype(F32) * own[...]
                own1[to, part] = kept.astype(BF16)
                total = total + jnp.sum(kept, axis=0, keepdims=True)
        small_ref[13:14, part] = total * scale

    if blocks:
        stage_z(1, 0)

    weight_term(own1, conv, None if blocks else gt1_ref, sums[0][0] if blocks else None)
    if blocks:
        stage_core(0)
        stage_z(1, 1)

    @pl.loop(0, ch // wide)
    def _(n):
        into[:, lanes(n, wide)] = lax.dot_general(
            back[...], w1_ref[lanes(n, wide), :], nt, preferred_element_type=F32
        ).astype(BF16)

    if blocks:
        stage_y(0)
        stage_z(1, 2)

    ss[...] = jnp.zeros_like(ss)
    pl.loop(0, groups)(lambda c: taps_back(c, 4, xp, fac, g1_ref, k1_ref, into, 0, 10))
    if blocks:
        small_sems = (small_send, small_recv)
        small_move = send(small_ref, srecv1, small_sems, 0, mate)
        stage_z(1, 3)
        stage_z(0, 0)
    f1 = fac[...]
    inner = jnp.sum(ss[...], axis=1, keepdims=True) * (1.0 / ch)
    ss[...] = f1 * f1 * f1 * jnp.broadcast_to(inner, f1.shape)
    def finish(c):
        part = lanes(c)
        for r in range(4):
            at = slice(r * rows, (r + 1) * rows)
            half = slice((r // 2) * rows, (r // 2 + 1) * rows)
            v = up[half, part] + fac[at] * dn[at, part] - xp[at, part] * ss[at]
            out_ref[at, part] = v.astype(BF16)

    middle = groups // 2
    pl.loop(0, middle)(finish)
    if blocks:
        small_move.wait()
        ssend2[...] = small_ref[...] + srecv1[...]
        small_move = send(ssend2, srecv2, small_sems, 1, over)
        stage_z(0, 1)
    pl.loop(middle, groups)(finish)
    if blocks:
        stage_z(0, 2)
        small_move.wait()
        sall[z] = ssend2[...] + srecv2[...]
        small_moves = [
            send(sall.at[z], sall.at[z], small_sems, 1 + s, hops[s][1]) for s in (1, 2, 3)
        ]
        stage_z(0, 3)
        stage_end(1, sum2_ref)
        stage_end(0, sum1_ref)
        for copy in small_moves:
            copy.wait()
        small_out[...] = (sall[0] + sall[1]) + (sall[2] + sall[3])
    else:
        small_out[...] = small_ref[...]


def tail_kernel(fast, p_ref, small_ref, *refs):
    if fast:
        s1_ref, s2_ref, x_out, w1_out, w2_out = refs[:5]
        refs = refs[5:]
    else:
        x_out, refs = refs[0], refs[1:]
    b1_out, b2_out, k1_out, k2_out, g1_out, g2_out, mix = refs
    batch, length, width = x_out.shape
    rows = p_ref.shape[0] // 4
    span = 4 * rows // batch
    ch = b1_out.shape[0]

    @pl.when(pl.program_id(0) == 0)
    def _():
        if fast:
            w1_out[...] = s1_ref[...]
            w2_out[...] = s2_ref[...]
        b1_out[...] = small_ref[13, :ch]
        b2_out[...] = small_ref[14, :]
        k1_out[...] = small_ref[0:5, :ch]
        k2_out[...] = small_ref[5:10, :ch]
        g1_out[...] = small_ref[10, :ch]
        g2_out[...] = small_ref[11, :ch]

    for k in range(width // LANES):
        part = slice(k * LANES, (k + 1) * LANES)
        for r in range(4):
            mix[k, pl.ds(r, rows, stride=4), :] = p_ref[r * rows : (r + 1) * rows, part].astype(F32)
        for b in range(batch):
            base = b * span + HALO
            x_out[b, :, part] = mix[k, base : base + length].astype(BF16)


def sums_scratch(ch, ch2, small_shape):
    shapes = []
    for size in (ch // 16, ch2 // 16):
        shapes += [
            pltpu.VMEM((2, 2, 4, size, ch), BF16),
            pltpu.VMEM((2, 4, size, ch), BF16),
            pltpu.VMEM((4, size, ch), F32),
            pltpu.VMEM((4, size, ch), BF16),
            pltpu.VMEM((4, size, ch), BF16),
            pltpu.VMEM((3, size, ch), BF16),
            pltpu.VMEM((3, size, ch), BF16),
            pltpu.SemaphoreType.DMA((9,)),
            pltpu.SemaphoreType.DMA((9,)),
        ]
    shapes += [pltpu.VMEM(small_shape, F32)] * 3 + [pltpu.VMEM((4,) + small_shape, F32)]
    return shapes + [pltpu.SemaphoreType.DMA((5,)), pltpu.SemaphoreType.DMA((5,))]


def per_device(fast, n, x, g1, k1, w1, b1, g2, k2, w2, b2, cot):
    batch, length, ch = x.shape
    quarter, ch2 = cot.shape[1:]
    scale = 1.0 / math.sqrt(batch * length * n)
    any_spec = pl.BlockSpec(memory_space=pl.ANY)
    vmem = pl.BlockSpec(memory_space=pltpu.VMEM)

    rows = batch * (length + 2 * HALO) // 4
    small_shape = (16, ch2)
    if fast:
        grads = [jax.ShapeDtypeStruct((k // 16, ch), F32) for k in (ch, ch2)]
    else:
        grads = [jax.ShapeDtypeStruct((ch, ch), F32), jax.ShapeDtypeStruct((ch2, ch), F32)]
    outs = pl.pallas_call(
        functools.partial(step_kernel, scale, n, fast),
        out_shape=[jax.ShapeDtypeStruct((4 * rows, ch), BF16)]
        + grads
        + [jax.ShapeDtypeStruct(small_shape, F32)],
        in_specs=[vmem] * 3 + [any_spec] + [vmem] * 3 + [any_spec] + [vmem] * 2,
        out_specs=[vmem] * (2 + len(grads)),
        scratch_shapes=[
            pltpu.VMEM((ch // LANES, 4 * rows, LANES), F32),
            pltpu.VMEM((4 * rows, ch), F32),
            pltpu.VMEM((4 * rows, LANES), F32),
            pltpu.VMEM((4 * rows, ch), BF16),
            pltpu.VMEM((4 * rows, ch), F32),
            pltpu.VMEM((2 * rows, ch), F32),
            pltpu.VMEM((2 * rows, LANES), F32),
            pltpu.VMEM((2 * rows, ch), BF16),
            pltpu.VMEM((2 * rows, ch2), BF16),
            pltpu.VMEM((2 * rows, ch2), BF16),
            pltpu.VMEM((2 * rows, ch), BF16),
            pltpu.VMEM((rows, ch2), F32),
            pltpu.VMEM((4 * rows, LANES), F32),
            pltpu.VMEM((rows, LANES), F32),
            pltpu.VMEM((rows, LANES), F32),
            pltpu.VMEM((4 * rows, ch), BF16),
            pltpu.VMEM((4 * rows, ch), BF16),
            pltpu.VMEM((4 * rows, ch), BF16),
            pltpu.VMEM((4 * rows, ch), F32),
            pltpu.VMEM((max(ch, ch2), ch), F32),
            pltpu.VMEM((batch, HALO, ch), BF16),
            pltpu.VMEM((batch, HALO, ch), BF16),
            pltpu.VMEM((batch, HALO, ch2), BF16),
            pltpu.VMEM((batch, HALO, ch2), BF16),
            pltpu.VMEM(w1.shape, BF16),
            pltpu.VMEM(w2.shape, BF16),
            pltpu.VMEM((1, ch), F32),
            pltpu.VMEM((1, ch), F32),
            pltpu.VMEM((1, ch), F32),
            pltpu.VMEM((1, ch2), F32),
            pltpu.VMEM(small_shape, F32),
            pltpu.SemaphoreType.DMA((4,)),
            pltpu.SemaphoreType.DMA((4,)),
            pltpu.SemaphoreType.DMA((2,)),
        ]
        + (sums_scratch(ch, ch2, small_shape) if fast else []),
        compiler_params=pltpu.CompilerParams(
            collective_id=0, has_side_effects=True, vmem_limit_bytes=58 * 2**20
        ),
        name="step",
    )(x, g1, k1, w1, b1, g2, k2, w2, b2, cot)
    planes, *parts, small = outs
    if not fast:
        grad_w = [
            lax.psum_scatter(part, "seq", scatter_dimension=0, tiled=True).T for part in parts
        ]
        small = lax.psum(small, "seq")
        parts = []

    def whole(shape):
        return pl.BlockSpec(shape, lambda i: (0,) * len(shape))

    width = 2 * LANES
    results = [part.shape for part in parts]
    results += [(ch,), (ch2,), (5, ch), (5, ch), (ch,), (ch,)]
    grad_x, *rest = pl.pallas_call(
        functools.partial(tail_kernel, fast),
        grid=(ch // width,),
        out_shape=[jax.ShapeDtypeStruct(x.shape, BF16)]
        + [jax.ShapeDtypeStruct(shape, F32) for shape in results],
        in_specs=[pl.BlockSpec((4 * rows, width), lambda i: (0, i)), whole(small_shape)]
        + [whole(part.shape) for part in parts],
        out_specs=[pl.BlockSpec((batch, length, width), lambda i: (0, 0, i))]
        + [whole(shape) for shape in results],
        scratch_shapes=[pltpu.VMEM((width // LANES, 4 * rows, LANES), F32)],
        name="tail",
    )(planes, small, *parts)
    if fast:
        grad_w, rest = [part.T for part in rest[:2]], rest[2:]
    return (grad_x, *grad_w, *rest)


def solution(mesh):
    n = mesh.shape["seq"]
    return jax.shard_map(
        functools.partial(per_device, n == 16, n),
        mesh=mesh,
        in_specs=(P("groups", "seq", None),) + (P(),) * 8 + (P("groups", "seq", None),),
        out_specs=(
            P("groups", "seq", None),
            P("groups", "seq"),
            P("groups", "seq"),
            P("groups"),
            P("groups"),
            P("groups", None),
            P("groups", None),
            P("groups"),
            P("groups"),
        ),
        check_vma=False,
    )
```
